256 devices in a mesh: dp: 4 (over z_lo, core), seq: 64 (over y, z_hi, x).
Axes of the slice: x: 4, y: 4, z: 8 (z_hi: 4, z_lo: 2; z = z_hi * 2 + z_lo), core: 2. Of those that a mesh axis runs over, the one named last changes fastest.
Arguments:
- activations: bfloat16 [4, 8192, 768], P('dp', 'seq'), may hold values from -600 to 600
- conv_weight: bfloat16 [3840, 768], replicated, may hold values from -0.09375 to 0.09375
- head_first: bfloat16 [768, 768], replicated, may hold values from -0.21875 to 0.21875
- head_second: bfloat16 [768], replicated, may hold values from -5 to 5
- hidden_cotangent: bfloat16 [4, 8192, 768], P('dp', 'seq'), may hold values from -3 to 3
- score_cotangent: float32 [4, 8192], P('dp', 'seq'), may hold values from -5 to 5
- donor_row: int32 [4, 8192], P('dp', 'seq'), may hold values from 0 to 127
- acceptor_owner: int32 [4, 8192, 1], P('dp', 'seq'), may hold values from 0 to 63; in each aligned block of 128 rows (0 to 127, 128 to 255, ..., all dimensions but the last counted through in order) at most 4 rows name the same one
- acceptor_row: int32 [4, 8192], P('dp', 'seq'), may hold values from 0 to 127
Outputs:
- input_grad: bfloat16 [4, 8192, 768], P('dp', 'seq')
- weight_grads: float32 [4608, 768], P('seq', 'dp')
The draws below stay inside these ranges and needn't reach their ends.
Inputs may be any that keep to these rules, and one draw needn't show every extreme that they name: `acceptor_owner`: among the 128 pairs of one block of positions, no block index is named by more than 4 pairs, a bound that some block reaches in every draw.
All inputs are finite; a program needn't handle non-finite values.
Results may differ from the reference program's by a relative error of at most 0.01.
Values may be sent and summed in bfloat16 or wider, within the bound.
No kernel may reach another device: no remote copies, remote signals or barrier semaphores. Data moves between devices by JAX's collectives and lax.ppermute only.
A program may use at most 64 MiB of HBM per device.

```python
import math
import jax
import jax.numpy as jnp
import numpy as np
from jax import lax

CHANNELS = 768
OUT_CHANNELS = 768
TAPS = 5
DILATION = 8
ROWS_DEV = 128
PAIRS_DEV = 128
BATCH = 4
SEQ_LEN = 8192
PAIRS = 8192
CAPACITY = 4
N_SEQ = 64


def draw_activations(key, part):
    key_base, key_rows, key_columns = jax.random.split(key, 3)
    shape_full = (BATCH, SEQ_LEN, CHANNELS)
    values = jnp.clip(jax.random.normal(key_base, shape_full, jnp.float32), -6.0, 6.0)
    row_scale = jnp.exp(jax.random.uniform(key_rows, (BATCH, SEQ_LEN, 1), jnp.float32, 0.0, math.log(10.0)))
    column_scale = jnp.exp(jax.random.uniform(key_columns, (1, 1, CHANNELS), jnp.float32, 0.0, math.log(10.0)))
    return (values * row_scale * column_scale).astype(jnp.bfloat16)


def place_ends(values, key, smallest, high):
    extent = values.shape
    place = [jax.random.randint(jax.random.fold_in(key, axis), (), 0, extent[axis]) for axis in range(len(extent))]
    values = values.at[tuple(place)].set(smallest)
    longest = extent.index(max(extent))
    place[longest] = (place[longest] + 1) % extent[longest]
    return values.at[tuple(place)].set(high)


def level_of(stream_key, shape, pieces, low, high):
    level, own = 1.0, jax.random.fold_in(stream_key, 6)
    for position, blocks in pieces:
        draws = jnp.exp(jax.random.uniform(jax.random.fold_in(own, position), (blocks,), jnp.float32, low / len(pieces), high / len(pieces)))
        level = level * jnp.repeat(draws, shape[position] // blocks).reshape([-1 if axis == position else 1 for axis in range(len(shape))])
    return level


def shared_out(own_key, own, number, rows, amount, top, reach, slope):
    ranking = jax.random.permutation(own_key, amount)
    crowded, usual = portions_of(amount, rows * top, reach, slope, True), portions_of(amount, rows * top, reach, slope, False)
    places = jnp.arange(amount)

    def named(tallies, offset_by):
        used = int((tallies > 0).sum())
        fixed = max(1, used // 4)
        shifted = fixed + (places - fixed + offset_by * (used - fixed)) % max(1, amount - fixed)
        return jnp.zeros((amount,), jnp.int32).at[ranking[jnp.where(places < fixed, places, shifted)]].set(jnp.asarray(tallies, jnp.int32))

    tallies = jnp.where(number % 4 == 0, named(crowded, number // 4), named(usual, number - number // 4 - 1))
    mixed = jax.random.permutation(jax.random.fold_in(own, 3), amount)
    source_of, taker = mixed[0:amount // 2 * 2:2], mixed[1:amount // 2 * 2:2]
    margin = jnp.minimum(tallies[source_of] - 1, reach - tallies[taker]) // 2
    margin = jnp.where((source_of == ranking[0]) | (taker == ranking[0]) | (tallies[taker] == 0), 0, jnp.maximum(margin, 0))
    shifted = jax.random.randint(jax.random.fold_in(own, 4), (amount // 2,), 0, 1 << 20) % (margin + 1)
    tallies = tallies.at[source_of].add(-shifted).at[taker].add(shifted)
    items = jnp.searchsorted(jnp.cumsum(tallies), jnp.arange(rows * top), side="right").astype(jnp.int32)
    table = items.reshape(top, rows).T
    table = table[jax.random.permutation(jax.random.fold_in(own, 1), rows)]
    offset_by = jax.random.randint(jax.random.fold_in(own, 2), (rows, 1), 0, top)
    return jnp.take_along_axis(table, (jnp.arange(top)[None, :] + offset_by) % top, axis=1)


def portions_of(count, total, most, lean, full):
    portions = [(1 << 20) // math.isqrt(rank ** lean) + 1 for rank in range(1, count + 1)]
    largest = most if full else min(most, max(-(-total // count), total * portions[0] // sum(portions)))
    least = 1 if total - largest >= count - 1 else 0
    holding, surplus = [largest] + [least] * (count - 1), total - largest - least * (count - 1)
    while surplus > 0:
        movable = [i for i in range(1, count) if holding[i] < largest] or [i for i in range(1, count) if holding[i] < most]
        mass, left = sum([portions[i] for i in movable]), surplus
        for i in movable:
            more = min(most - holding[i], max(1, left * portions[i] // mass), surplus)
            holding[i] = holding[i] + more
            surplus = surplus - more
    return np.array(holding)


def gaussian(rng, extent, spread, bound, shards=(), kind=jnp.bfloat16):
    entries = spread * jax.random.normal(rng, extent, jnp.float32)
    if shards:
        entries = entries * level_of(rng, extent, shards, -0.22, 0.18)
    return jnp.clip(entries, -bound, bound).astype(kind)


def setup_inputs(seed: int = 0) -> dict:
    splits = jax.random.split(jax.random.key(seed), 10)
    activations = draw_activations(jax.random.fold_in(splits[9], 71), 0)
    conv_weight = gaussian(splits[1], (TAPS * CHANNELS, OUT_CHANNELS), (TAPS * CHANNELS) ** -0.5, 0.09375)
    head_first = gaussian(splits[2], (OUT_CHANNELS, OUT_CHANNELS), OUT_CHANNELS ** -0.5, 0.21875)
    head_second = gaussian(splits[3], (OUT_CHANNELS,), 1.0, 5.0)
    hidden_cotangent = gaussian(splits[4], (BATCH, SEQ_LEN, OUT_CHANNELS), 0.5, 3.0, ((0, 4), (1, 64)))
    score_cotangent = gaussian(splits[5], (BATCH, PAIRS), 1.0, 5.0, ((0, 4), (1, 64)), jnp.float32)
    donor_row = place_ends(jax.random.randint(splits[6], (BATCH, PAIRS), 0, ROWS_DEV), jax.random.fold_in(splits[6], 1), 0, ROWS_DEV - 1).astype(jnp.int32)
    acceptor_owner_keys = jax.random.split(jax.random.fold_in(splits[7], 1), BATCH * PAIRS // PAIRS_DEV)
    acceptor_owner_turns = jax.random.permutation(jax.random.fold_in(splits[7], 3), BATCH * PAIRS // PAIRS_DEV)
    acceptor_owner = jax.vmap(lambda own, number: shared_out(jax.random.fold_in(splits[7], 2), own, number, PAIRS_DEV, N_SEQ, 1, CAPACITY, 2))(acceptor_owner_keys, acceptor_owner_turns).reshape((BATCH, PAIRS, 1))
    acceptor_row = place_ends(jax.random.randint(splits[8], (BATCH, PAIRS), 0, ROWS_DEV), jax.random.fold_in(splits[8], 1), 0, ROWS_DEV - 1).astype(jnp.int32)
    return dict(activations=activations, conv_weight=conv_weight, head_first=head_first, head_second=head_second, hidden_cotangent=hidden_cotangent, score_cotangent=score_cotangent, donor_row=donor_row, acceptor_owner=acceptor_owner, acceptor_row=acceptor_row)


def gelu_slope(values):
    normal_cdf = 0.5 * (1.0 + lax.erf(values * (1.0 / math.sqrt(2.0))))
    density = jnp.exp(-0.5 * values * values) * (1.0 / math.sqrt(2.0 * math.pi))
    return normal_cdf + values * density

def contract_rows(left_side, right_side):
    return lax.dot_general(left_side, right_side, (((0,), (0,)), ((), ())), preferred_element_type=jnp.float32)

def reference(activations, conv_weight, head_first, head_second, hidden_cotangent, score_cotangent, donor_row, acceptor_owner, acceptor_row):
    reach_rows = (TAPS - 1) // 2 * DILATION
    shard_of_pair = jnp.arange(PAIRS, dtype=jnp.int32) // PAIRS_DEV
    conv_total = jnp.zeros((TAPS * CHANNELS, OUT_CHANNELS), jnp.float32)
    head_total = jnp.zeros((OUT_CHANNELS, OUT_CHANNELS), jnp.float32)
    grads_out = []
    for batch_index in range(BATCH):
        input_values = activations[batch_index].astype(jnp.float32)
        norm_inverse = lax.rsqrt(lax.optimization_barrier(jnp.mean(input_values * input_values, axis=1, keepdims=True)) + 1e-05)
        normed = (input_values * norm_inverse).astype(jnp.bfloat16)
        padded = jnp.pad(normed, ((reach_rows, reach_rows), (0, 0)))
        preact = jnp.zeros((SEQ_LEN, OUT_CHANNELS), jnp.float32)
        for tap_index in range(TAPS):
            first_row = tap_index * DILATION
            preact = preact + jnp.dot(padded[first_row:first_row + SEQ_LEN], conv_weight[tap_index * CHANNELS:(tap_index + 1) * CHANNELS], preferred_element_type=jnp.float32)
        hidden = jax.nn.gelu(preact, approximate=False).astype(jnp.bfloat16)
        donor_pos = (shard_of_pair * ROWS_DEV + donor_row[batch_index]).astype(jnp.int32)
        accept_pos = (acceptor_owner[batch_index, :, 0] * ROWS_DEV + acceptor_row[batch_index]).astype(jnp.int32)
        donor_values = hidden[donor_pos].astype(jnp.float32)
        accept_values = hidden[accept_pos].astype(jnp.float32)
        pair_feature = (donor_values * accept_values).astype(jnp.bfloat16)
        head_preact = jnp.dot(pair_feature, head_first, preferred_element_type=jnp.float32)
        head_delta = (score_cotangent[batch_index][:, None] * head_second.astype(jnp.float32)[None, :] * gelu_slope(head_preact)).astype(jnp.bfloat16)
        feature_grad = lax.dot_general(head_delta, head_first, (((1,), (1,)), ((), ())), preferred_element_type=jnp.float32)
        donor_grad = (feature_grad * accept_values).astype(jnp.bfloat16)
        accept_grad = (feature_grad * donor_values).astype(jnp.bfloat16)
        hidden_grad = hidden_cotangent[batch_index].astype(jnp.float32)
        hidden_grad = hidden_grad.at[donor_pos].add(donor_grad.astype(jnp.float32))
        hidden_grad = hidden_grad.at[accept_pos].add(accept_grad.astype(jnp.float32))
        preact_grad = (hidden_grad * gelu_slope(preact)).astype(jnp.bfloat16)
        grad_padded = jnp.pad(preact_grad, ((reach_rows, reach_rows), (0, 0)))
        normed_grad = jnp.zeros((SEQ_LEN, CHANNELS), jnp.float32)
        for tap_index in range(TAPS):
            first_row = 2 * reach_rows - tap_index * DILATION
            normed_grad = normed_grad + lax.dot_general(grad_padded[first_row:first_row + SEQ_LEN], conv_weight[tap_index * CHANNELS:(tap_index + 1) * CHANNELS], (((1,), (1,)), ((), ())), preferred_element_type=jnp.float32)
        input_grad = norm_inverse * normed_grad - input_values * norm_inverse ** 3 * lax.optimization_barrier(jnp.mean(normed_grad * input_values, axis=1, keepdims=True))
        grads_out.append(input_grad.astype(jnp.bfloat16))
        conv_parts = [contract_rows(padded[tap_index * DILATION:tap_index * DILATION + SEQ_LEN], preact_grad) for tap_index in range(TAPS)]
        conv_total = conv_total + jnp.concatenate(conv_parts, axis=0)
        head_total = head_total + contract_rows(pair_feature, head_delta)
    weight_grads = jnp.concatenate([conv_total * (1.0 / math.sqrt(BATCH * SEQ_LEN)), head_total * (1.0 / math.sqrt(BATCH * PAIRS))], axis=0)
    return (jnp.stack(grads_out), weight_grads)
```

```python
import math

import jax
import jax.numpy as jnp
from jax import lax
from jax.sharding import PartitionSpec as P

DILATION = 8


def gelu_slope(values):
    normal_cdf = 0.5 * (1.0 + lax.erf(values * (1.0 / math.sqrt(2.0))))
    density = jnp.exp(-0.5 * values * values) * (1.0 / math.sqrt(2.0 * math.pi))
    return normal_cdf + values * density


def contract_rows(left_side, right_side):
    return lax.dot_general(
        left_side, right_side, (((0,), (0,)), ((), ())), preferred_element_type=jnp.float32
    )


def seq_halo(cells, width):
    count = lax.axis_size("seq")
    above = lax.ppermute(cells[-width:], "seq", [(i, i + 1) for i in range(count - 1)])
    below = lax.ppermute(cells[:width], "seq", [(i + 1, i) for i in range(count - 1)])
    return above, below


def swap_core(field):
    return lax.ppermute(field, "dp", [(0, 1), (1, 0), (2, 3), (3, 2)])


def swap_z(field):
    return lax.ppermute(field, "dp", [(0, 2), (1, 3), (2, 0), (3, 1)])


def dp_peers(field):
    core = swap_core(field)
    z_side = swap_z(field)
    return field, core, z_side, swap_core(z_side)


def dp_columns(field, width):
    index = lax.axis_index("dp")
    found = []
    for flip in range(4):
        piece = lax.dynamic_slice_in_dim(field, (index ^ flip) * width, width, axis=1)
        if flip:
            piece = lax.ppermute(piece, "dp", [(i, i ^ flip) for i in range(4)])
        found.append(piece)
    return found


def per_device(
    activations,
    conv_weight,
    head_first,
    head_second,
    hidden_cotangent,
    score_cotangent,
    donor_row,
    acceptor_owner,
    acceptor_row,
):
    row_count = activations.shape[1]
    chan_count = activations.shape[2]
    out_count = conv_weight.shape[1]
    tap_count = conv_weight.shape[0] // chan_count
    reach_rows = (tap_count - 1) // 2 * DILATION
    shards = lax.axis_size("seq")
    dp_count = lax.axis_size("dp")
    pair_count = donor_row.shape[1]
    capacity = max(2, 2 * pair_count // shards)
    slots = shards * capacity
    col_width = out_count // dp_count

    above, below = seq_halo(activations[0], reach_rows)
    owner = acceptor_owner[0, :, 0]
    pair_ids = jnp.arange(pair_count, dtype=jnp.int32)
    rank = jnp.sum(
        ((owner[:, None] == owner[None, :]) & (pair_ids[None, :] < pair_ids[:, None])).astype(
            jnp.int32
        ),
        axis=1,
    )
    target = owner * capacity + rank
    placed = target[:, None] == jnp.arange(slots, dtype=jnp.int32)[None, :]

    def to_slots(values, empty):
        return jnp.sum(jnp.where(placed, (values - empty)[:, None], 0.0), axis=0) + empty

    score_slot = jnp.sum(jnp.where(placed, score_cotangent[0][:, None], 0.0), axis=0)
    accept_slot = to_slots(acceptor_row[0].astype(jnp.float32), -1.0)
    donor_slot = to_slots(donor_row[0].astype(jnp.float32), -1.0)
    ask = jnp.concatenate(
        [accept_slot.reshape(shards, capacity), score_slot.reshape(shards, capacity)], axis=1
    )
    asked = lax.all_to_all(ask, "seq", split_axis=0, concat_axis=0, tiled=True)

    padded_input = jnp.concatenate([above, activations[0], below], axis=0)
    padded_peers = dp_peers(padded_input)

    def normalise(field):
        values = field.astype(jnp.float32)
        inverse = lax.rsqrt(jnp.mean(values * values, axis=1, keepdims=True) + 1e-05)
        return values, inverse, (values * inverse).astype(jnp.bfloat16)

    padded_values, padded_inverse, padded = normalise(padded_input)
    input_values = padded_values[reach_rows : reach_rows + row_count]
    norm_inverse = padded_inverse[reach_rows : reach_rows + row_count]

    def tap_columns(field):
        return jnp.concatenate(
            [field[k * DILATION : k * DILATION + row_count] for k in range(tap_count)], axis=1
        )

    columns = tap_columns(padded)
    preact = jnp.dot(columns, conv_weight, preferred_element_type=jnp.float32)
    hidden = jax.nn.gelu(preact, approximate=False).astype(jnp.bfloat16)

    row_ids = jnp.arange(row_count, dtype=jnp.int32).astype(jnp.float32)
    own_rows = jnp.concatenate(
        [donor_slot.reshape(shards, capacity), asked[:, :capacity]], axis=1
    ).reshape(2 * slots)
    own_scores = jnp.concatenate(
        [score_slot.reshape(shards, capacity), asked[:, capacity:]], axis=1
    ).reshape(2 * slots)
    hits = (row_ids[:, None] == own_rows[None, :]).astype(jnp.bfloat16)
    sent = contract_rows(hits, hidden).astype(jnp.bfloat16)
    got = lax.all_to_all(
        sent.reshape(shards, 2 * capacity, out_count), "seq", split_axis=0, concat_axis=0, tiled=True
    )
    partner = jnp.concatenate([got[:, capacity:], got[:, :capacity]], axis=1).reshape(
        2 * slots, out_count
    )
    partner_values = partner.astype(jnp.float32)
    pair_feature = (sent.astype(jnp.float32) * partner_values).astype(jnp.bfloat16)

    def own_pairs(field):
        halves = field.reshape(shards, 2 * capacity, out_count)[:, :capacity].reshape(
            slots, out_count
        )
        return jnp.dot(placed.astype(jnp.bfloat16), halves, preferred_element_type=jnp.float32).astype(
            jnp.bfloat16
        )

    feature_peers = dp_peers(own_pairs(pair_feature))
    head_preact = jnp.dot(pair_feature, head_first, preferred_element_type=jnp.float32)
    head_delta = (
        own_scores[:, None] * head_second.astype(jnp.float32)[None, :] * gelu_slope(head_preact)
    ).astype(jnp.bfloat16)
    delta_peers = dp_columns(own_pairs(head_delta), col_width)
    feature_grad = lax.dot_general(
        head_delta, head_first, (((1,), (1,)), ((), ())), preferred_element_type=jnp.float32
    )
    row_grad = (feature_grad * partner_values).astype(jnp.bfloat16)
    hidden_grad = hidden_cotangent[0].astype(jnp.float32) + jnp.dot(
        hits, row_grad, preferred_element_type=jnp.float32
    )
    preact_grad = (hidden_grad * gelu_slope(preact)).astype(jnp.bfloat16)

    grad_peers = dp_columns(preact_grad, col_width)
    grad_above, grad_below = seq_halo(preact_grad, reach_rows)

    columns_all = jnp.concatenate(
        [columns] + [tap_columns(normalise(peer)[2]) for peer in padded_peers[1:]], axis=0
    )
    conv_term = contract_rows(columns_all, jnp.concatenate(grad_peers, axis=0)) * (
        1.0 / math.sqrt(dp_count * row_count * shards)
    )
    head_term = contract_rows(
        jnp.concatenate(feature_peers, axis=0), jnp.concatenate(delta_peers, axis=0)
    ) * (1.0 / math.sqrt(dp_count * pair_count * shards))
    term = jnp.concatenate([conv_term.astype(jnp.bfloat16), head_term.astype(jnp.bfloat16)], axis=0)
    share = term.shape[0] // shards
    terms = lax.all_to_all(
        term.reshape(shards, share, col_width), "seq", split_axis=0, concat_axis=0, tiled=True
    )
    weight_grads = jnp.sum(terms.astype(jnp.float32), axis=0)

    grad_padded = jnp.concatenate([grad_above, preact_grad, grad_below], axis=0)
    spread = lax.dot_general(
        grad_padded, conv_weight, (((1,), (1,)), ((), ())), preferred_element_type=jnp.float32
    )
    normed_grad = spread[2 * reach_rows : 2 * reach_rows + row_count, 0:chan_count]
    for tap_index in range(1, tap_count):
        first_row = 2 * reach_rows - tap_index * DILATION
        normed_grad = (
            normed_grad
            + spread[
                first_row : first_row + row_count,
                tap_index * chan_count : (tap_index + 1) * chan_count,
            ]
        )
    input_grad = norm_inverse * normed_grad - input_values * norm_inverse**3 * jnp.mean(
        normed_grad * input_values, axis=1, keepdims=True
    )
    return (input_grad.astype(jnp.bfloat16)[None], weight_grads)


def solution(mesh):
    placed = (
        P("dp", "seq", None),
        P(),
        P(),
        P(),
        P("dp", "seq", None),
        P("dp", "seq"),
        P("dp", "seq"),
        P("dp", "seq", None),
        P("dp", "seq"),
    )
    return jax.shard_map(
        per_device,
        mesh=mesh,
        in_specs=placed,
        out_specs=(P("dp", "seq", None), P("seq", "dp")),
        check_vma=False,
    )
```

```python
import functools
import math

import jax
import jax.numpy as jnp
from jax import lax
from jax.experimental import pallas as pl
from jax.experimental.pallas import tpu as pltpu
from jax.sharding import PartitionSpec as P


DILATION = 8


def gelu_slope(values):
    normal_cdf = 0.5 * (1.0 + lax.erf(values * (1.0 / math.sqrt(2.0))))
    density = jnp.exp(-0.5 * values * values) * (1.0 / math.sqrt(2.0 * math.pi))
    return normal_cdf + values * density


def contract_rows(left_side, right_side):
    return lax.dot_general(
        left_side, right_side, (((0,), (0,)), ((), ())), preferred_element_type=jnp.float32
    )


def seq_halo(cells, width):
    count = lax.axis_size("seq")
    above = lax.ppermute(cells[-width:], "seq", [(i, i + 1) for i in range(count - 1)])
    below = lax.ppermute(cells[:width], "seq", [(i + 1, i) for i in range(count - 1)])
    return above, below


def swap_core(field):
    return lax.ppermute(field, "dp", [(0, 1), (1, 0), (2, 3), (3, 2)])


def swap_z(field):
    return lax.ppermute(field, "dp", [(0, 2), (1, 3), (2, 0), (3, 1)])


def dp_peers(field):
    core = swap_core(field)
    z_side = swap_z(field)
    return field, core, z_side, swap_core(z_side)


def dp_columns(field, width):
    index = lax.axis_index("dp")
    found = []
    for flip in range(4):
        piece = lax.dynamic_slice_in_dim(field, (index ^ flip) * width, width, axis=1)
        if flip:
            piece = lax.ppermute(piece, "dp", [(i, i ^ flip) for i in range(4)])
        found.append(piece)
    return found


def weight_kernel(scale, taps, *refs):
    normed_ref, out_ref = refs[0], refs[-1]
    grads, features, deltas = refs[1:5], refs[5:9], refs[9:13]
    chan_count = normed_ref.shape[0]
    width = grads[0].shape[1]
    reach = (taps - 1) * DILATION
    values = [ref[...].astype(jnp.float32) for ref in grads]
    for k in range(taps):
        pieces = []
        for value in values:
            if k:
                pieces.append(jnp.zeros((k * DILATION, width), jnp.float32))
            pieces.append(value)
            if k < taps - 1:
                pieces.append(jnp.zeros((reach - k * DILATION, width), jnp.float32))
        shifted = jnp.concatenate(pieces, axis=0).astype(jnp.bfloat16)
        term = jnp.dot(normed_ref[...], shifted, preferred_element_type=jnp.float32)
        out_ref[k * chan_count : (k + 1) * chan_count, :] = (term * scale).astype(jnp.bfloat16)
    term = contract_rows(
        jnp.concatenate([ref[...] for ref in features], axis=0),
        jnp.concatenate([ref[...] for ref in deltas], axis=0),
    )
    out_ref[taps * chan_count :, :] = (term * scale).astype(jnp.bfloat16)


def per_device(
    activations,
    conv_weight,
    head_first,
    head_second,
    hidden_cotangent,
    score_cotangent,
    donor_row,
    acceptor_owner,
    acceptor_row,
):
    row_count = activations.shape[1]
    chan_count = activations.shape[2]
    out_count = conv_weight.shape[1]
    tap_count = conv_weight.shape[0] // chan_count
    reach_rows = (tap_count - 1) // 2 * DILATION
    shards = lax.axis_size("seq")
    dp_count = lax.axis_size("dp")
    pair_count = donor_row.shape[1]
    capacity = max(2, 2 * pair_count // shards)
    slots = shards * capacity
    col_width = out_count // dp_count

    above, below = seq_halo(activations[0], reach_rows)
    owner = acceptor_owner[0, :, 0]
    pair_ids = jnp.arange(pair_count, dtype=jnp.int32)
    rank = jnp.sum(
        ((owner[:, None] == owner[None, :]) & (pair_ids[None, :] < pair_ids[:, None])).astype(
            jnp.int32
        ),
        axis=1,
    )
    target = owner * capacity + rank
    placed = target[:, None] == jnp.arange(slots, dtype=jnp.int32)[None, :]

    def to_slots(values, empty):
        return jnp.sum(jnp.where(placed, (values - empty)[:, None], 0.0), axis=0) + empty

    score_slot = jnp.sum(jnp.where(placed, score_cotangent[0][:, None], 0.0), axis=0)
    accept_slot = to_slots(acceptor_row[0].astype(jnp.float32), -1.0)
    donor_slot = to_slots(donor_row[0].astype(jnp.float32), -1.0)
    ask = jnp.concatenate(
        [accept_slot.reshape(shards, capacity), score_slot.reshape(shards, capacity)], axis=1
    )
    asked = lax.all_to_all(ask, "seq", split_axis=0, concat_axis=0, tiled=True)

    padded_input = jnp.concatenate([above, activations[0], below], axis=0)
    padded_peers = dp_peers(padded_input)

    def normalise(field):
        values = field.astype(jnp.float32)
        inverse = lax.rsqrt(jnp.mean(values * values, axis=1, keepdims=True) + 1e-05)
        return values, inverse, (values * inverse).astype(jnp.bfloat16)

    _, padded_inverse, padded = normalise(padded_input)
    norm_inverse = padded_inverse[reach_rows : reach_rows + row_count]

    def tap_columns(field):
        return jnp.concatenate(
            [field[k * DILATION : k * DILATION + row_count] for k in range(tap_count)], axis=1
        )

    columns = tap_columns(padded)
    preact = jnp.dot(columns, conv_weight, preferred_element_type=jnp.float32)
    hidden = jax.nn.gelu(preact, approximate=False).astype(jnp.bfloat16)
    slope = gelu_slope(preact)
    hidden, slope = lax.optimization_barrier((hidden, slope))

    row_ids = jnp.arange(row_count, dtype=jnp.int32).astype(jnp.float32)
    own_rows = jnp.concatenate(
        [donor_slot.reshape(shards, capacity), asked[:, :capacity]], axis=1
    ).reshape(2 * slots)
    own_scores = jnp.concatenate(
        [score_slot.reshape(shards, capacity), asked[:, capacity:]], axis=1
    ).reshape(2 * slots)
    hits = (row_ids[:, None] == own_rows[None, :]).astype(jnp.bfloat16)
    sent = contract_rows(hits, hidden).astype(jnp.bfloat16)
    got = lax.all_to_all(
        sent.reshape(shards, 2 * capacity, out_count), "seq", split_axis=0, concat_axis=0, tiled=True
    )
    partner = jnp.concatenate([got[:, capacity:], got[:, :capacity]], axis=1).reshape(
        2 * slots, out_count
    )
    partner_values = partner.astype(jnp.float32)
    pair_feature = (sent.astype(jnp.float32) * partner_values).astype(jnp.bfloat16)

    def own_pairs(field):
        halves = field.reshape(shards, 2 * capacity, out_count)[:, :capacity].reshape(
            slots, out_count
        )
        return jnp.dot(placed.astype(jnp.bfloat16), halves, preferred_element_type=jnp.float32).astype(
            jnp.bfloat16
        )

    feature_peers = dp_peers(own_pairs(pair_feature))
    head_preact = jnp.dot(pair_feature, head_first, preferred_element_type=jnp.float32)
    head_delta = (
        own_scores[:, None] * head_second.astype(jnp.float32)[None, :] * gelu_slope(head_preact)
    ).astype(jnp.bfloat16)
    delta_peers = dp_columns(own_pairs(head_delta), col_width)
    feature_grad = lax.dot_general(
        head_delta, head_first, (((1,), (1,)), ((), ())), preferred_element_type=jnp.float32
    )
    row_grad = (feature_grad * partner_values).astype(jnp.bfloat16)
    hidden_grad = hidden_cotangent[0].astype(jnp.float32) + jnp.dot(
        hits, row_grad, preferred_element_type=jnp.float32
    )
    preact_grad = (hidden_grad * slope).astype(jnp.bfloat16)

    grad_peers = dp_columns(preact_grad, col_width)
    grad_above, grad_below = seq_halo(preact_grad, reach_rows)

    normed_all = jnp.concatenate(
        [padded] + [normalise(peer)[2] for peer in padded_peers[1:]], axis=0
    ).T
    term = pl.pallas_call(
        functools.partial(
            weight_kernel, 1.0 / math.sqrt(dp_count * row_count * shards), tap_count
        ),
        out_shape=jax.ShapeDtypeStruct(
            (tap_count * chan_count + out_count, col_width), jnp.bfloat16
        ),
        in_specs=[pl.BlockSpec(memory_space=pltpu.VMEM)] * 13,
        out_specs=pl.BlockSpec(memory_space=pltpu.VMEM),
    )(normed_all, *grad_peers, *feature_peers, *delta_peers)
    term, grad_above, grad_below, norm_inverse = lax.optimization_barrier(
        (term, grad_above, grad_below, norm_inverse)
    )
    share = term.shape[0] // shards
    terms = lax.all_to_all(
        term.reshape(shards, share, col_width), "seq", split_axis=0, concat_axis=0, tiled=True
    )
    terms, grad_above, grad_below, late_input, norm_inverse = lax.optimization_barrier(
        (terms, grad_above, grad_below, activations[0], norm_inverse)
    )
    input_values = late_input.astype(jnp.float32)
    weight_grads = jnp.sum(terms.astype(jnp.float32), axis=0)

    grad_padded = jnp.concatenate([grad_above, preact_grad, grad_below], axis=0)
    spread = lax.dot_general(
        grad_padded, conv_weight, (((1,), (1,)), ((), ())), preferred_element_type=jnp.float32
    )
    normed_grad = spread[2 * reach_rows : 2 * reach_rows + row_count, 0:chan_count]
    for tap_index in range(1, tap_count):
        first_row = 2 * reach_rows - tap_index * DILATION
        normed_grad = (
            normed_grad
            + spread[
                first_row : first_row + row_count,
                tap_index * chan_count : (tap_index + 1) * chan_count,
            ]
        )
    input_grad = norm_inverse * normed_grad - input_values * norm_inverse**3 * jnp.mean(
        normed_grad * input_values, axis=1, keepdims=True
    )
    return (input_grad.astype(jnp.bfloat16)[None], weight_grads)


def solution(mesh):
    placed = (
        P("dp", "seq", None),
        P(),
        P(),
        P(),
        P("dp", "seq", None),
        P("dp", "seq"),
        P("dp", "seq"),
        P("dp", "seq", None),
        P("dp", "seq"),
    )

    return jax.shard_map(
        per_device,
        mesh=mesh,
        in_specs=placed,
        out_specs=(P("dp", "seq", None), P("seq", "dp")),
        check_vma=False,
    )
```

```python
import functools
import math

import jax
import jax.numpy as jnp
from jax import lax
from jax.experimental import pallas as pl
from jax.experimental.pallas import tpu as pltpu
from jax.sharding import PartitionSpec as P


DILATION = 8
LANES = 128
KERNEL_VMEM = 16 * 1024 * 1024


def gelu_slope(values):
    normal_cdf = 0.5 * (1.0 + lax.erf(values * (1.0 / math.sqrt(2.0))))
    density = jnp.exp(-0.5 * values * values) * (1.0 / math.sqrt(2.0 * math.pi))
    return normal_cdf + values * density


def contract_rows(left_side, right_side):
    return lax.dot_general(
        left_side, right_side, (((0,), (0,)), ((), ())), preferred_element_type=jnp.float32
    )


def seq_halo(cells, width):
    count = lax.axis_size("seq")
    above = lax.ppermute(cells[-width:], "seq", [(i, i + 1) for i in range(count - 1)])
    below = lax.ppermute(cells[:width], "seq", [(i + 1, i) for i in range(count - 1)])
    return above, below


def swap_core(field):
    return lax.ppermute(field, "dp", [(0, 1), (1, 0), (2, 3), (3, 2)])


def swap_z(field):
    return lax.ppermute(field, "dp", [(0, 2), (1, 3), (2, 0), (3, 1)])


def dp_peers(field):
    core = swap_core(field)
    z_side = swap_z(field)
    return field, core, z_side, swap_core(z_side)


def dp_columns(field, width):
    index = lax.axis_index("dp")
    found = []
    for flip in range(4):
        piece = lax.dynamic_slice_in_dim(field, (index ^ flip) * width, width, axis=1)
        if flip:
            piece = lax.ppermute(piece, "dp", [(i, i ^ flip) for i in range(4)])
        found.append(piece)
    return found


def pair_kernel(got_ref, hidden_ref, first_ref, second_ref, cotangent_ref, *outs):
    back_ref, part_ref, feature_ref, delta_ref = outs
    chan_count = hidden_ref.shape[1]
    slots = got_ref.shape[0]
    note = got_ref[:, chan_count:].astype(jnp.float32)
    score = note[:, 1:2] + note[:, 2:3] + note[:, 3:4]
    row_ids = lax.broadcasted_iota(jnp.int32, (slots, hidden_ref.shape[0]), 1).astype(jnp.float32)
    hits = (note[:, 0:1] == row_ids).astype(jnp.float32).astype(jnp.bfloat16)
    accept = jnp.dot(hits, hidden_ref[...], preferred_element_type=jnp.float32)
    donor = got_ref[:, :chan_count].astype(jnp.float32)
    feature = (donor * accept).astype(jnp.bfloat16)
    feature_ref[...] = feature
    head_preact = jnp.dot(feature, first_ref[...], preferred_element_type=jnp.float32)
    delta = (score * second_ref[...].astype(jnp.float32) * gelu_slope(head_preact)).astype(
        jnp.bfloat16
    )
    delta_ref[...] = delta
    feature_grad = lax.dot_general(
        delta, first_ref[...], (((1,), (1,)), ((), ())), preferred_element_type=jnp.float32
    )
    back_ref[...] = (feature_grad * accept).astype(jnp.bfloat16)
    accept_grad = (feature_grad * donor).astype(jnp.bfloat16)
    part_ref[...] = cotangent_ref[...].astype(jnp.float32) + contract_rows(hits, accept_grad)


def head_kernel(scale, *refs):
    term = contract_rows(refs[0][...], refs[4][...])
    for feature, delta in zip(refs[1:4], refs[5:8], strict=True):
        term = term + contract_rows(feature[...], delta[...])
    refs[8][...] = (term * scale).astype(jnp.bfloat16)


def weight_kernel(scale, taps, *refs):
    normed_ref, head_ref, grads, out_ref = refs[0], refs[1], refs[2:6], refs[6]
    chan_count = normed_ref.shape[0]
    width = grads[0].shape[1]
    reach = (taps - 1) * DILATION
    values = [ref[...].astype(jnp.float32) for ref in grads]
    for k in range(taps):
        pieces = []
        for value in values:
            if k:
                pieces.append(jnp.zeros((k * DILATION, width), jnp.float32))
            pieces.append(value)
            if k < taps - 1:
                pieces.append(jnp.zeros((reach - k * DILATION, width), jnp.float32))
        shifted = jnp.concatenate(pieces, axis=0).astype(jnp.bfloat16)
        term = jnp.dot(normed_ref[...], shifted, preferred_element_type=jnp.float32)
        out_ref[k * chan_count : (k + 1) * chan_count, :] = (term * scale).astype(jnp.bfloat16)
    out_ref[taps * chan_count :, :] = head_ref[...]


def in_vmem(kernel, shapes, count, limit):
    spec = pl.BlockSpec(memory_space=pltpu.VMEM)
    return pl.pallas_call(
        kernel,
        out_shape=shapes,
        in_specs=[spec] * count,
        out_specs=jax.tree.map(lambda _: spec, shapes),
        compiler_params=pltpu.CompilerParams(vmem_limit_bytes=limit),
    )


def per_device(
    activations,
    conv_weight,
    head_first,
    head_second,
    hidden_cotangent,
    score_cotangent,
    donor_row,
    acceptor_owner,
    acceptor_row,
):
    row_count = activations.shape[1]
    chan_count = activations.shape[2]
    out_count = conv_weight.shape[1]
    tap_count = conv_weight.shape[0] // chan_count
    reach_rows = (tap_count - 1) // 2 * DILATION
    shards = lax.axis_size("seq")
    dp_count = lax.axis_size("dp")
    pair_count = donor_row.shape[1]
    capacity = max(2, 2 * pair_count // shards)
    slots = shards * capacity
    col_width = out_count // dp_count

    above, below = seq_halo(activations[0], reach_rows)
    owner = acceptor_owner[0, :, 0]
    pair_ids = jnp.arange(pair_count, dtype=jnp.int32)
    rank = jnp.sum(
        ((owner[:, None] == owner[None, :]) & (pair_ids[None, :] < pair_ids[:, None])).astype(
            jnp.int32
        ),
        axis=1,
    )
    target = owner * capacity + rank
    placed = target[None, :] == jnp.arange(slots, dtype=jnp.int32)[:, None]
    score = score_cotangent[0]
    high = lax.reduce_precision(score, 8, 7)
    middle = lax.reduce_precision(score - high, 8, 7)
    note = jnp.stack([acceptor_row[0].astype(jnp.float32) + 1.0, high, middle, score - high - middle])
    note = jnp.pad(note, ((0, LANES - note.shape[0]), (0, 0))).astype(jnp.bfloat16)
    notes = lax.dot_general(
        placed.astype(jnp.bfloat16), note, (((1,), (1,)), ((), ())), preferred_element_type=jnp.float32
    )
    notes = (notes - (jnp.arange(LANES) == 0).astype(jnp.float32)[None, :]).astype(jnp.bfloat16)
    donor_slot = (
        jnp.sum(jnp.where(placed, donor_row[0][None, :] + 1, 0), axis=1, dtype=jnp.int32) - 1
    )
    row_ids = jnp.arange(row_count, dtype=jnp.int32)
    hits = (donor_slot[:, None] == row_ids[None, :]).astype(jnp.bfloat16)
    hits, notes = lax.optimization_barrier((hits, notes))

    padded_input = jnp.concatenate([above, activations[0], below], axis=0)
    padded_peers = dp_peers(padded_input)

    def normalise(field):
        values = field.astype(jnp.float32)
        inverse = lax.rsqrt(jnp.mean(values * values, axis=1, keepdims=True) + 1e-05)
        return values, inverse, (values * inverse).astype(jnp.bfloat16)

    _, padded_inverse, padded = normalise(padded_input)
    norm_inverse = padded_inverse[reach_rows : reach_rows + row_count]

    def tap_columns(field):
        return jnp.concatenate(
            [field[k * DILATION : k * DILATION + row_count] for k in range(tap_count)], axis=1
        )

    columns = tap_columns(padded)
    preact = jnp.dot(columns, conv_weight, preferred_element_type=jnp.float32)
    hidden = jax.nn.gelu(preact, approximate=False).astype(jnp.bfloat16)
    slope = gelu_slope(preact)
    hidden, slope = lax.optimization_barrier((hidden, slope))

    sent = jnp.concatenate(
        [jnp.dot(hits, hidden, preferred_element_type=jnp.float32).astype(jnp.bfloat16), notes], axis=1
    )
    got = lax.all_to_all(
        sent.reshape(shards, capacity, out_count + LANES),
        "seq",
        split_axis=0,
        concat_axis=0,
        tiled=True,
    ).reshape(slots, out_count + LANES)
    slot_shape = jax.ShapeDtypeStruct((slots, out_count), jnp.bfloat16)
    back, part, feature, delta = in_vmem(
        pair_kernel,
        (
            slot_shape,
            jax.ShapeDtypeStruct((row_count, out_count), jnp.float32),
            slot_shape,
            slot_shape,
        ),
        5,
        KERNEL_VMEM,
    )(got, hidden, head_first, head_second.reshape(1, out_count), hidden_cotangent[0])
    donor_grad = lax.all_to_all(
        back.reshape(shards, capacity, out_count),
        "seq",
        split_axis=0,
        concat_axis=0,
        tiled=True,
    ).reshape(slots, out_count)
    feature_peers = dp_peers(feature)
    delta_peers = dp_columns(delta, col_width)
    head_term = in_vmem(
        functools.partial(head_kernel, 1.0 / math.sqrt(dp_count * pair_count * shards)),
        jax.ShapeDtypeStruct((out_count, col_width), jnp.bfloat16),
        8,
        KERNEL_VMEM,
    )(*feature_peers, *delta_peers)
    hidden_grad = part + contract_rows(hits, donor_grad)
    preact_grad = (hidden_grad * slope).astype(jnp.bfloat16)

    grad_peers = dp_columns(preact_grad, col_width)
    grad_above, grad_below = seq_halo(preact_grad, reach_rows)

    normed_all = jnp.concatenate(
        [padded] + [normalise(peer)[2] for peer in padded_peers[1:]], axis=0
    ).T
    term = in_vmem(
        functools.partial(
            weight_kernel, 1.0 / math.sqrt(dp_count * row_count * shards), tap_count
        ),
        jax.ShapeDtypeStruct((tap_count * chan_count + out_count, col_width), jnp.bfloat16),
        6,
        KERNEL_VMEM,
    )(normed_all, head_term, *grad_peers)
    term, grad_above, grad_below, norm_inverse = lax.optimization_barrier(
        (term, grad_above, grad_below, norm_inverse)
    )
    share = term.shape[0] // shards
    terms = lax.all_to_all(
        term.reshape(shards, share, col_width), "seq", split_axis=0, concat_axis=0, tiled=True
    )
    terms, grad_above, grad_below, late_input, norm_inverse = lax.optimization_barrier(
        (terms, grad_above, grad_below, activations[0], norm_inverse)
    )
    input_values = late_input.astype(jnp.float32)
    weight_grads = jnp.sum(terms.astype(jnp.float32), axis=0)

    grad_padded = jnp.concatenate([grad_above, preact_grad, grad_below], axis=0)
    spread = lax.dot_general(
        grad_padded, conv_weight, (((1,), (1,)), ((), ())), preferred_element_type=jnp.float32
    )
    normed_grad = spread[2 * reach_rows : 2 * reach_rows + row_count, 0:chan_count]
    for tap_index in range(1, tap_count):
        first_row = 2 * reach_rows - tap_index * DILATION
        normed_grad = (
            normed_grad
            + spread[
                first_row : first_row + row_count,
                tap_index * chan_count : (tap_index + 1) * chan_count,
            ]
        )
    input_grad = norm_inverse * normed_grad - input_values * norm_inverse**3 * jnp.mean(
        normed_grad * input_values, axis=1, keepdims=True
    )
    return (input_grad.astype(jnp.bfloat16)[None], weight_grads)


def solution(mesh):
    placed = (
        P("dp", "seq", None),
        P(),
        P(),
        P(),
        P("dp", "seq", None),
        P("dp", "seq"),
        P("dp", "seq"),
        P("dp", "seq", None),
        P("dp", "seq"),
    )

    return jax.shard_map(
        per_device,
        mesh=mesh,
        in_specs=placed,
        out_specs=(P("dp", "seq", None), P("seq", "dp")),
        check_vma=False,
    )
```

```python
import functools
import math

import jax
import jax.numpy as jnp
from jax import lax
from jax.experimental import pallas as pl
from jax.experimental.pallas import tpu as pltpu
from jax.sharding import PartitionSpec as P


DILATION = 8
LANES = 128
KERNEL_VMEM = 16 * 1024 * 1024


def gelu_slope(values):
    normal_cdf = 0.5 * (1.0 + lax.erf(values * (1.0 / math.sqrt(2.0))))
    density = jnp.exp(-0.5 * values * values) * (1.0 / math.sqrt(2.0 * math.pi))
    return normal_cdf + values * density


def contract_rows(left_side, right_side):
    return lax.dot_general(
        left_side, right_side, (((0,), (0,)), ((), ())), preferred_element_type=jnp.float32
    )


def seq_halo(cells, width):
    count = lax.axis_size("seq")
    above = lax.ppermute(cells[-width:], "seq", [(i, i + 1) for i in range(count - 1)])
    below = lax.ppermute(cells[:width], "seq", [(i + 1, i) for i in range(count - 1)])
    return above, below


def swap_core(field):
    return lax.ppermute(field, "dp", [(0, 1), (1, 0), (2, 3), (3, 2)])


def swap_z(field):
    return lax.ppermute(field, "dp", [(0, 2), (1, 3), (2, 0), (3, 1)])


def dp_peers(field):
    core = swap_core(field)
    z_side = swap_z(field)
    return field, core, z_side, swap_core(z_side)


def dp_columns(field, width):
    index = lax.axis_index("dp")
    found = []
    for flip in range(4):
        piece = lax.dynamic_slice_in_dim(field, (index ^ flip) * width, width, axis=1)
        if flip:
            piece = lax.ppermute(piece, "dp", [(i, i ^ flip) for i in range(4)])
        found.append(piece)
    return found


def pair_kernel(got_ref, hidden_ref, first_ref, second_ref, cotangent_ref, *outs):
    back_ref, part_ref, feature_ref, delta_ref = outs
    chan_count = hidden_ref.shape[1]
    slots = got_ref.shape[0]
    note = got_ref[:, chan_count:].astype(jnp.float32)
    score = note[:, 1:2] + note[:, 2:3] + note[:, 3:4]
    row_ids = lax.broadcasted_iota(jnp.int32, (slots, hidden_ref.shape[0]), 1).astype(jnp.float32)
    hits = (note[:, 0:1] == row_ids).astype(jnp.float32).astype(jnp.bfloat16)
    accept = jnp.dot(hits, hidden_ref[...], preferred_element_type=jnp.float32)
    donor = got_ref[:, :chan_count].astype(jnp.float32)
    feature = (donor * accept).astype(jnp.bfloat16)
    feature_ref[...] = feature
    head_preact = jnp.dot(feature, first_ref[...], preferred_element_type=jnp.float32)
    delta = (score * second_ref[...].astype(jnp.float32) * gelu_slope(head_preact)).astype(
        jnp.bfloat16
    )
    delta_ref[...] = delta
    feature_grad = lax.dot_general(
        delta, first_ref[...], (((1,), (1,)), ((), ())), preferred_element_type=jnp.float32
    )
    back_ref[...] = (feature_grad * accept).astype(jnp.bfloat16)
    accept_grad = (feature_grad * donor).astype(jnp.bfloat16)
    part_ref[...] = cotangent_ref[...].astype(jnp.float32) + contract_rows(hits, accept_grad)


def head_kernel(scale, *refs):
    term = contract_rows(refs[4][...], refs[0][...])
    for feature, delta in zip(refs[1:4], refs[5:8], strict=True):
        term = term + contract_rows(delta[...], feature[...])
    refs[8][...] = (term * scale).astype(jnp.bfloat16)


def weight_kernel(scale, taps, *refs):
    normed, head_ref, grads, out_ref = refs[0:4], refs[4], refs[5:9], refs[9]
    chan_count = normed[0].shape[1]
    width = grads[0].shape[1]
    reach = (taps - 1) * DILATION
    piece = out_ref.shape[2]
    inputs = jnp.concatenate([ref[...] for ref in normed], axis=0)
    values = [ref[...].astype(jnp.float32) for ref in grads]

    def put(first, block):
        done = 0
        while done < block.shape[1]:
            part, inside = divmod(first + done, piece)
            step = min(piece - inside, block.shape[1] - done)
            out_ref[part, :, inside : inside + step] = block[:, done : done + step]
            done += step

    for k in range(taps):
        pieces = []
        for value in values:
            if k:
                pieces.append(jnp.zeros((k * DILATION, width), jnp.float32))
            pieces.append(value)
            if k < taps - 1:
                pieces.append(jnp.zeros((reach - k * DILATION, width), jnp.float32))
        shifted = jnp.concatenate(pieces, axis=0).astype(jnp.bfloat16)
        term = contract_rows(shifted, inputs)
        put(k * chan_count, (term * scale).astype(jnp.bfloat16))
    put(taps * chan_count, head_ref[...])


def fold_kernel(terms_ref, out_ref):
    total = terms_ref[0].astype(jnp.float32)
    for index in range(1, terms_ref.shape[0]):
        total = total + terms_ref[index].astype(jnp.float32)
    out_ref[...] = total.T.astype(jnp.bfloat16)


def in_vmem(kernel, shapes, count, limit):
    spec = pl.BlockSpec(memory_space=pltpu.VMEM)
    return pl.pallas_call(
        kernel,
        out_shape=shapes,
        in_specs=[spec] * count,
        out_specs=jax.tree.map(lambda _: spec, shapes),
        compiler_params=pltpu.CompilerParams(vmem_limit_bytes=limit),
    )


def per_device(
    activations,
    conv_weight,
    head_first,
    head_second,
    hidden_cotangent,
    score_cotangent,
    donor_row,
    acceptor_owner,
    acceptor_row,
):
    row_count = activations.shape[1]
    chan_count = activations.shape[2]
    out_count = conv_weight.shape[1]
    tap_count = conv_weight.shape[0] // chan_count
    reach_rows = (tap_count - 1) // 2 * DILATION
    shards = lax.axis_size("seq")
    dp_count = lax.axis_size("dp")
    pair_count = donor_row.shape[1]
    capacity = max(2, 2 * pair_count // shards)
    slots = shards * capacity
    col_width = out_count // dp_count

    above, below = seq_halo(activations[0], reach_rows)
    owner = acceptor_owner[0, :, 0]
    pair_ids = jnp.arange(pair_count, dtype=jnp.int32)
    rank = jnp.sum(
        ((owner[:, None] == owner[None, :]) & (pair_ids[None, :] < pair_ids[:, None])).astype(
            jnp.int32
        ),
        axis=1,
    )
    target = owner * capacity + rank
    placed = target[None, :] == jnp.arange(slots, dtype=jnp.int32)[:, None]
    score = score_cotangent[0]
    high = lax.reduce_precision(score, 8, 7)
    middle = lax.reduce_precision(score - high, 8, 7)
    note = jnp.stack([acceptor_row[0].astype(jnp.float32) + 1.0, high, middle, score - high - middle])
    note = jnp.pad(note, ((0, LANES - note.shape[0]), (0, 0))).astype(jnp.bfloat16)
    notes = lax.dot_general(
        placed.astype(jnp.bfloat16), note, (((1,), (1,)), ((), ())), preferred_element_type=jnp.float32
    )
    notes = (notes - (jnp.arange(LANES) == 0).astype(jnp.float32)[None, :]).astype(jnp.bfloat16)
    donor_slot = (
        jnp.sum(jnp.where(placed, donor_row[0][None, :] + 1, 0), axis=1, dtype=jnp.int32) - 1
    )
    row_ids = jnp.arange(row_count, dtype=jnp.int32)
    hits = (donor_slot[:, None] == row_ids[None, :]).astype(jnp.bfloat16)
    hits, notes = lax.optimization_barrier((hits, notes))

    padded_input = jnp.concatenate([above, activations[0], below], axis=0)
    padded_peers = dp_peers(padded_input)

    def normalise(field):
        values = field.astype(jnp.float32)
        inverse = lax.rsqrt(jnp.mean(values * values, axis=1, keepdims=True) + 1e-05)
        return values, inverse, (values * inverse).astype(jnp.bfloat16)

    _, padded_inverse, padded = normalise(padded_input)
    norm_inverse = padded_inverse[reach_rows : reach_rows + row_count]

    def tap_columns(field):
        return jnp.concatenate(
            [field[k * DILATION : k * DILATION + row_count] for k in range(tap_count)], axis=1
        )

    columns = tap_columns(padded)
    preact = jnp.dot(columns, conv_weight, preferred_element_type=jnp.float32)
    hidden = jax.nn.gelu(preact, approximate=False).astype(jnp.bfloat16)
    slope = gelu_slope(preact)
    hidden, slope = lax.optimization_barrier((hidden, slope))

    sent = jnp.concatenate(
        [jnp.dot(hits, hidden, preferred_element_type=jnp.float32).astype(jnp.bfloat16), notes], axis=1
    )
    got = lax.all_to_all(
        sent.reshape(shards, capacity, out_count + LANES),
        "seq",
        split_axis=0,
        concat_axis=0,
        tiled=True,
    ).reshape(slots, out_count + LANES)
    slot_shape = jax.ShapeDtypeStruct((slots, out_count), jnp.bfloat16)
    back, part, feature, delta = in_vmem(
        pair_kernel,
        (
            slot_shape,
            jax.ShapeDtypeStruct((row_count, out_count), jnp.float32),
            slot_shape,
            slot_shape,
        ),
        5,
        KERNEL_VMEM,
    )(got, hidden, head_first, head_second.reshape(1, out_count), hidden_cotangent[0])
    donor_grad = lax.all_to_all(
        back.reshape(shards, capacity, out_count),
        "seq",
        split_axis=0,
        concat_axis=0,
        tiled=True,
    ).reshape(slots, out_count)
    feature_peers = dp_peers(feature)
    delta_peers = dp_columns(delta, col_width)
    head_term = in_vmem(
        functools.partial(head_kernel, 1.0 / math.sqrt(dp_count * pair_count * shards)),
        jax.ShapeDtypeStruct((col_width, out_count), jnp.bfloat16),
        8,
        KERNEL_VMEM,
    )(*feature_peers, *delta_peers)
    hidden_grad = part + contract_rows(hits, donor_grad)
    preact_grad = (hidden_grad * slope).astype(jnp.bfloat16)

    grad_peers = dp_columns(preact_grad, col_width)

    normed_peers = [padded] + [normalise(peer)[2] for peer in padded_peers[1:]]
    row_total = tap_count * chan_count + out_count
    outer = 4
    inner = shards // outer
    term = in_vmem(
        functools.partial(
            weight_kernel, 1.0 / math.sqrt(dp_count * row_count * shards), tap_count
        ),
        jax.ShapeDtypeStruct((outer, col_width, row_total // outer), jnp.bfloat16),
        9,
        KERNEL_VMEM,
    )(*normed_peers, head_term, *grad_peers)
    terms = lax.all_to_all(
        term,
        "seq",
        split_axis=0,
        concat_axis=0,
        tiled=True,
        axis_index_groups=[[i + j * inner for j in range(outer)] for i in range(inner)],
    )
    terms, halo_source = lax.optimization_barrier((terms, preact_grad))
    folded = in_vmem(
        fold_kernel,
        jax.ShapeDtypeStruct((row_total // outer, col_width), jnp.bfloat16),
        1,
        KERNEL_VMEM,
    )(terms)
    shares = lax.all_to_all(
        folded.reshape(inner, row_total // shards, col_width),
        "seq",
        split_axis=0,
        concat_axis=0,
        tiled=True,
        axis_index_groups=[[j * inner + i for i in range(inner)] for j in range(outer)],
    )
    weight_grads = jnp.sum(shares.astype(jnp.float32), axis=0)

    input_grad = data_grad(
        activations[0], norm_inverse, halo_source, conv_weight, reach_rows, tap_count
    )
    return (input_grad.astype(jnp.bfloat16)[None], weight_grads)


def data_grad(inputs, norm_inverse, preact_grad, conv_weight, reach_rows, tap_count):
    row_count, chan_count = inputs.shape
    input_values = inputs.astype(jnp.float32)
    grad_above, grad_below = seq_halo(preact_grad, reach_rows)
    grad_padded = jnp.concatenate([grad_above, preact_grad, grad_below], axis=0)
    spread = lax.dot_general(
        grad_padded, conv_weight, (((1,), (1,)), ((), ())), preferred_element_type=jnp.float32
    )
    normed_grad = spread[2 * reach_rows : 2 * reach_rows + row_count, 0:chan_count]
    for tap_index in range(1, tap_count):
        first_row = 2 * reach_rows - tap_index * DILATION
        normed_grad = (
            normed_grad
            + spread[
                first_row : first_row + row_count,
                tap_index * chan_count : (tap_index + 1) * chan_count,
            ]
        )
    return norm_inverse * normed_grad - input_values * norm_inverse**3 * jnp.mean(
        normed_grad * input_values, axis=1, keepdims=True
    )


def solution(mesh):
    placed = (
        P("dp", "seq", None),
        P(),
        P(),
        P(),
        P("dp", "seq", None),
        P("dp", "seq"),
        P("dp", "seq"),
        P("dp", "seq", None),
        P("dp", "seq"),
    )

    return jax.shard_map(
        per_device,
        mesh=mesh,
        in_specs=placed,
        out_specs=(P("dp", "seq", None), P("seq", "dp")),
        check_vma=False,
    )
```

```python
import functools
import math

import jax
import jax.numpy as jnp
from jax import lax
from jax.experimental import pallas as pl
from jax.experimental.pallas import tpu as pltpu
from jax.sharding import PartitionSpec as P


DILATION = 8
LANES = 128
SEQ_GRID = (4, 4, 4)
KERNEL_VMEM = 16 * 1024 * 1024


def gelu_slope(values):
    normal_cdf = 0.5 * (1.0 + lax.erf(values * (1.0 / math.sqrt(2.0))))
    density = jnp.exp(-0.5 * values * values) * (1.0 / math.sqrt(2.0 * math.pi))
    return normal_cdf + values * density


def contract_rows(left_side, right_side):
    return lax.dot_general(
        left_side, right_side, (((0,), (0,)), ((), ())), preferred_element_type=jnp.float32
    )


def seq_halo(cells, width):
    count = lax.axis_size("seq")
    above = lax.ppermute(cells[-width:], "seq", [(i, i + 1) for i in range(count - 1)])
    below = lax.ppermute(cells[:width], "seq", [(i + 1, i) for i in range(count - 1)])
    return above, below


def swap_core(field):
    return lax.ppermute(field, "dp", [(0, 1), (1, 0), (2, 3), (3, 2)])


def swap_z(field):
    return lax.ppermute(field, "dp", [(0, 2), (1, 3), (2, 0), (3, 1)])


def dp_peers(field):
    core = swap_core(field)
    z_side = swap_z(field)
    return field, core, z_side, swap_core(z_side)


def dp_exchange(pieces):
    return [pieces[0]] + [
        lax.ppermute(pieces[flip], "dp", [(i, i ^ flip) for i in range(4)]) for flip in range(1, 4)
    ]


def split_columns(values, place, blocks_ref, outs):
    tiles = [values[:, i * LANES : (i + 1) * LANES] for i in range(values.shape[1] // LANES)]
    turned = [pltpu.roll(tile, LANES // 2, axis=1) for tile in tiles]
    low = lax.broadcasted_iota(jnp.int32, tiles[0].shape, 1) < LANES // 2
    for pair in range(2):
        first, middle, last = range(3 * pair, 3 * pair + 3)
        blocks = (
            (tiles[first], jnp.where(low, tiles[middle], turned[middle])),
            (
                jnp.where(low, turned[middle], turned[last]),
                jnp.where(low, turned[last], tiles[last]),
            ),
        )
        for side, halves in enumerate(blocks):
            blocks_ref[2 * pair + side] = jnp.concatenate(halves, axis=1).astype(jnp.bfloat16)
    for flip, out in enumerate(outs):
        out[...] = blocks_ref[place ^ flip]


def grad_kernel(place_ref, hits_ref, back_ref, part_ref, slope_ref, grad_ref, *rest):
    hidden_grad = part_ref[...] + contract_rows(hits_ref[...], back_ref[...])
    grad = hidden_grad * slope_ref[...]
    grad_ref[...] = grad.astype(jnp.bfloat16)
    split_columns(grad, place_ref[0], rest[-1], rest[:-1])


def pair_kernel(place_ref, got_ref, hidden_ref, first_ref, second_ref, cotangent_ref, *outs):
    back_ref, part_ref, feature_ref = outs[:3]
    chan_count = hidden_ref.shape[1]
    slots = got_ref.shape[0]
    note = got_ref[:, chan_count:].astype(jnp.float32)
    score = note[:, 1:2] + note[:, 2:3] + note[:, 3:4]
    row_ids = lax.broadcasted_iota(jnp.int32, (slots, hidden_ref.shape[0]), 1).astype(jnp.float32)
    hits = (note[:, 0:1] == row_ids).astype(jnp.float32).astype(jnp.bfloat16)
    accept = jnp.dot(hits, hidden_ref[...], preferred_element_type=jnp.float32)
    donor = got_ref[:, :chan_count].astype(jnp.float32)
    feature = (donor * accept).astype(jnp.bfloat16)
    feature_ref[...] = feature
    head_preact = jnp.dot(feature, first_ref[...], preferred_element_type=jnp.float32)
    delta = score * second_ref[...].astype(jnp.float32) * gelu_slope(head_preact)
    split_columns(delta, place_ref[0], outs[-1], outs[3:-1])
    delta = delta.astype(jnp.bfloat16)
    feature_grad = lax.dot_general(
        delta, first_ref[...], (((1,), (1,)), ((), ())), preferred_element_type=jnp.float32
    )
    back_ref[...] = (feature_grad * accept).astype(jnp.bfloat16)
    accept_grad = (feature_grad * donor).astype(jnp.bfloat16)
    part_ref[...] = cotangent_ref[...].astype(jnp.float32) + contract_rows(hits, accept_grad)


def head_kernel(scale, *refs):
    term = contract_rows(refs[0][...], refs[4][...])
    for feature, delta in zip(refs[1:4], refs[5:8], strict=True):
        term = term + contract_rows(feature[...], delta[...])
    refs[8][...] = (term * scale).astype(jnp.bfloat16)


def weight_kernel(scale, taps, grid, *refs):
    normed_ref, head_ref, grads, out_ref, tail_ref = refs[0], refs[1], refs[2:6], refs[6], refs[7]
    ys, zs, xs = grid
    chan_count = normed_ref.shape[0]
    width = grads[0].shape[1]
    reach = (taps - 1) * DILATION
    share = tail_ref.shape[0] // (ys * zs * xs)
    chunk = share * zs + share * zs // 2
    values = [ref[...].astype(jnp.float32) for ref in grads]

    def put(first, block):
        tail_ref[first : first + block.shape[0], :] = block[:, LANES:]
        done = 0
        while done < block.shape[0]:
            owner, inside = divmod(first + done, share)
            step = min(share - inside, block.shape[0] - done)
            y, z, x = owner // (zs * xs), owner // xs % zs, owner % xs
            start = (y * xs + x) * chunk + z * share + inside
            out_ref[start : start + step, :] = block[done : done + step, :LANES].astype(jnp.bfloat16)
            done += step

    for k in range(taps):
        pieces = []
        for value in values:
            if k:
                pieces.append(jnp.zeros((k * DILATION, width), jnp.float32))
            pieces.append(value)
            if k < taps - 1:
                pieces.append(jnp.zeros((reach - k * DILATION, width), jnp.float32))
        shifted = jnp.concatenate(pieces, axis=0).astype(jnp.bfloat16)
        put(
            k * chan_count,
            jnp.dot(normed_ref[...], shifted, preferred_element_type=jnp.float32) * scale,
        )
    put(taps * chan_count, head_ref[...].astype(jnp.float32))
    low = lax.broadcasted_iota(jnp.int32, (share, LANES), 1) < LANES // 2
    for y in range(ys):
        for x in range(xs):
            for z in range(zs // 2):
                rows = [((y * zs + half) * xs + x) * share for half in (z, z + zs // 2)]
                start = (y * xs + x) * chunk + (zs + z) * share
                out_ref[start : start + share, :] = jnp.where(
                    low, tail_ref[rows[0] : rows[0] + share, :], tail_ref[rows[1] : rows[1] + share, :]
                ).astype(jnp.bfloat16)


def fold_kernel(share, zs, terms_ref, out_ref):
    total = terms_ref[0].astype(jnp.float32)
    for index in range(1, terms_ref.shape[0]):
        total = total + terms_ref[index].astype(jnp.float32)
    for z in range(zs):
        out_ref[z, :share, :] = total[z * share : (z + 1) * share].astype(jnp.bfloat16)
        first = (zs + z % (zs // 2)) * share
        out_ref[z, share:, :] = total[first : first + share].astype(jnp.bfloat16)


def in_vmem(kernel, shapes, count, limit, scratch=(), scalars=0):
    spec = pl.BlockSpec(memory_space=pltpu.VMEM)
    scalar = pl.BlockSpec(memory_space=pltpu.SMEM)
    return pl.pallas_call(
        kernel,
        out_shape=shapes,
        in_specs=[scalar] * scalars + [spec] * count,
        out_specs=jax.tree.map(lambda _: spec, shapes),
        scratch_shapes=scratch,
        compiler_params=pltpu.CompilerParams(vmem_limit_bytes=limit),
    )


def per_device(
    activations,
    conv_weight,
    head_first,
    head_second,
    hidden_cotangent,
    score_cotangent,
    donor_row,
    acceptor_owner,
    acceptor_row,
):
    row_count = activations.shape[1]
    chan_count = activations.shape[2]
    out_count = conv_weight.shape[1]
    tap_count = conv_weight.shape[0] // chan_count
    reach_rows = (tap_count - 1) // 2 * DILATION
    shards = lax.axis_size("seq")
    dp_count = lax.axis_size("dp")
    pair_count = donor_row.shape[1]
    capacity = max(2, 2 * pair_count // shards)
    slots = shards * capacity

    above, below = seq_halo(activations[0], reach_rows)
    owner = acceptor_owner[0, :, 0]
    pair_ids = jnp.arange(pair_count, dtype=jnp.int32)
    rank = jnp.sum(
        ((owner[:, None] == owner[None, :]) & (pair_ids[None, :] < pair_ids[:, None])).astype(
            jnp.int32
        ),
        axis=1,
    )
    target = owner * capacity + rank
    placed = target[None, :] == jnp.arange(slots, dtype=jnp.int32)[:, None]
    score = score_cotangent[0]
    high = lax.reduce_precision(score, 8, 7)
    middle = lax.reduce_precision(score - high, 8, 7)
    note = jnp.stack([acceptor_row[0].astype(jnp.float32) + 1.0, high, middle, score - high - middle])
    note = jnp.pad(note, ((0, LANES - note.shape[0]), (0, 0))).astype(jnp.bfloat16)
    notes = lax.dot_general(
        placed.astype(jnp.bfloat16), note, (((1,), (1,)), ((), ())), preferred_element_type=jnp.float32
    )
    notes = (notes - (jnp.arange(LANES) == 0).astype(jnp.float32)[None, :]).astype(jnp.bfloat16)
    donor_slot = (
        jnp.sum(jnp.where(placed, donor_row[0][None, :] + 1, 0), axis=1, dtype=jnp.int32) - 1
    )
    row_ids = jnp.arange(row_count, dtype=jnp.int32)
    hits = (donor_slot[:, None] == row_ids[None, :]).astype(jnp.bfloat16)
    hits, notes = lax.optimization_barrier((hits, notes))

    padded_input = jnp.concatenate([above, activations[0], below], axis=0)
    padded_peers = dp_peers(padded_input)

    def normalise(field):
        values = field.astype(jnp.float32)
        inverse = lax.rsqrt(jnp.mean(values * values, axis=1, keepdims=True) + 1e-05)
        return values, inverse, (values * inverse).astype(jnp.bfloat16)

    _, padded_inverse, padded = normalise(padded_input)
    norm_inverse = padded_inverse[reach_rows : reach_rows + row_count]

    def tap_columns(field):
        return jnp.concatenate(
            [field[k * DILATION : k * DILATION + row_count] for k in range(tap_count)], axis=1
        )

    columns = tap_columns(padded)
    preact = jnp.dot(columns, conv_weight, preferred_element_type=jnp.float32)
    hidden = jax.nn.gelu(preact, approximate=False).astype(jnp.bfloat16)
    slope = gelu_slope(preact)
    hidden, slope = lax.optimization_barrier((hidden, slope))

    sent = jnp.concatenate(
        [jnp.dot(hits, hidden, preferred_element_type=jnp.float32).astype(jnp.bfloat16), notes], axis=1
    )
    got = lax.all_to_all(
        sent.reshape(shards, capacity, out_count + LANES),
        "seq",
        split_axis=0,
        concat_axis=0,
        tiled=True,
    ).reshape(slots, out_count + LANES)
    slot_shape = jax.ShapeDtypeStruct((slots, out_count), jnp.bfloat16)
    place = lax.axis_index("dp").astype(jnp.int32).reshape(1)
    back, part, feature, *delta = in_vmem(
        pair_kernel,
        (slot_shape, jax.ShapeDtypeStruct((row_count, out_count), jnp.float32), slot_shape)
        + (jax.ShapeDtypeStruct((slots, 2 * LANES), jnp.bfloat16),) * dp_count,
        5,
        KERNEL_VMEM,
        [pltpu.VMEM((dp_count, slots, 2 * LANES), jnp.bfloat16)],
        1,
    )(place, got, hidden, head_first, head_second.reshape(1, out_count), hidden_cotangent[0])
    donor_grad = lax.all_to_all(
        back.reshape(shards, capacity, out_count),
        "seq",
        split_axis=0,
        concat_axis=0,
        tiled=True,
    ).reshape(slots, out_count)
    feature_peers = dp_peers(feature)
    delta_peers = dp_exchange(delta)
    head_term = in_vmem(
        functools.partial(head_kernel, 1.0 / math.sqrt(dp_count * pair_count * shards)),
        jax.ShapeDtypeStruct((out_count, 2 * LANES), jnp.bfloat16),
        8,
        KERNEL_VMEM,
    )(*feature_peers, *delta_peers)
    preact_grad, *grads = in_vmem(
        grad_kernel,
        (jax.ShapeDtypeStruct((row_count, out_count), jnp.bfloat16),)
        + (jax.ShapeDtypeStruct((row_count, 2 * LANES), jnp.bfloat16),) * dp_count,
        4,
        KERNEL_VMEM,
        [pltpu.VMEM((dp_count, row_count, 2 * LANES), jnp.bfloat16)],
        1,
    )(place, hits, donor_grad, part, slope)
    grad_peers = dp_exchange(grads)

    normed_all = jnp.concatenate(
        [padded] + [normalise(peer)[2] for peer in padded_peers[1:]], axis=0
    ).T
    ys, zs, xs = SEQ_GRID
    row_total = tap_count * chan_count + out_count
    share = row_total // shards
    chunk = share * zs + share * zs // 2
    term = in_vmem(
        functools.partial(
            weight_kernel, 1.0 / math.sqrt(dp_count * row_count * shards), tap_count, SEQ_GRID
        ),
        jax.ShapeDtypeStruct((ys * xs * chunk, LANES), jnp.bfloat16),
        6,
        KERNEL_VMEM,
        [pltpu.VMEM((row_total, LANES), jnp.float32)],
    )(normed_all, head_term, *grad_peers)
    terms = lax.all_to_all(
        term.reshape(ys * xs, chunk, LANES),
        "seq",
        split_axis=0,
        concat_axis=0,
        tiled=True,
        axis_index_groups=[
            [(y * zs + z) * xs + x for y in range(ys) for x in range(xs)] for z in range(zs)
        ],
    )
    terms, halo_source = lax.optimization_barrier((terms, preact_grad))
    folded = in_vmem(
        functools.partial(fold_kernel, share, zs),
        jax.ShapeDtypeStruct((zs, 2 * share, LANES), jnp.bfloat16),
        1,
        KERNEL_VMEM,
    )(terms)
    shares = lax.all_to_all(
        folded,
        "seq",
        split_axis=0,
        concat_axis=0,
        tiled=True,
        axis_index_groups=[
            [(y * zs + z) * xs + x for z in range(zs)] for y in range(ys) for x in range(xs)
        ],
    )
    total = jnp.sum(shares.astype(jnp.float32), axis=0)
    upper = lax.axis_index("seq") // xs % zs >= zs // 2
    others = jnp.where(upper, total[share:, LANES // 2 :], total[share:, : LANES // 2])
    weight_grads = jnp.concatenate([total[:share], others], axis=1)

    input_grad = data_grad(
        activations[0], norm_inverse, halo_source, conv_weight, reach_rows, tap_count
    )
    return (input_grad.astype(jnp.bfloat16)[None], weight_grads)


def data_grad(inputs, norm_inverse, preact_grad, conv_weight, reach_rows, tap_count):
    row_count, chan_count = inputs.shape
    input_values = inputs.astype(jnp.float32)
    grad_above, grad_below = seq_halo(preact_grad, reach_rows)
    grad_padded = jnp.concatenate([grad_above, preact_grad, grad_below], axis=0)
    spread = lax.dot_general(
        grad_padded, conv_weight, (((1,), (1,)), ((), ())), preferred_element_type=jnp.float32
    )
    normed_grad = spread[2 * reach_rows : 2 * reach_rows + row_count, 0:chan_count]
    for tap_index in range(1, tap_count):
        first_row = 2 * reach_rows - tap_index * DILATION
        normed_grad = (
            normed_grad
            + spread[
                first_row : first_row + row_count,
                tap_index * chan_count : (tap_index + 1) * chan_count,
            ]
        )
    return norm_inverse * normed_grad - input_values * norm_inverse**3 * jnp.mean(
        normed_grad * input_values, axis=1, keepdims=True
    )


def solution(mesh):
    placed = (
        P("dp", "seq", None),
        P(),
        P(),
        P(),
        P("dp", "seq", None),
        P("dp", "seq"),
        P("dp", "seq"),
        P("dp", "seq", None),
        P("dp", "seq"),
    )

    return jax.shard_map(
        per_device,
        mesh=mesh,
        in_specs=placed,
        out_specs=(P("dp", "seq", None), P("seq", "dp")),
        check_vma=False,
    )
```

```python
import functools
import math

import jax
import jax.numpy as jnp
from jax import lax
from jax.experimental import pallas as pl
from jax.experimental.pallas import tpu as pltpu
from jax.sharding import PartitionSpec as P


DILATION = 8
LANES = 128
SEQ_GRID = (4, 4, 4)
KERNEL_VMEM = 16 * 1024 * 1024


def gelu_slope(values):
    normal_cdf = 0.5 * (1.0 + lax.erf(values * (1.0 / math.sqrt(2.0))))
    density = jnp.exp(-0.5 * values * values) * (1.0 / math.sqrt(2.0 * math.pi))
    return normal_cdf + values * density


def contract_rows(left_side, right_side):
    return lax.dot_general(
        left_side, right_side, (((0,), (0,)), ((), ())), preferred_element_type=jnp.float32
    )


def seq_halo(cells, width):
    count = lax.axis_size("seq")
    above = lax.ppermute(cells[-width:], "seq", [(i, i + 1) for i in range(count - 1)])
    below = lax.ppermute(cells[:width], "seq", [(i + 1, i) for i in range(count - 1)])
    return above, below


def swap_core(field):
    return lax.ppermute(field, "dp", [(0, 1), (1, 0), (2, 3), (3, 2)])


def swap_z(field):
    return lax.ppermute(field, "dp", [(0, 2), (1, 3), (2, 0), (3, 1)])


def dp_peers(field):
    core = swap_core(field)
    z_side = swap_z(field)
    return field, core, z_side, swap_core(z_side)


def dp_columns(field, width):
    index = lax.axis_index("dp")
    found = []
    for flip in range(4):
        piece = lax.dynamic_slice_in_dim(field, (index ^ flip) * width, width, axis=1)
        if flip:
            piece = lax.ppermute(piece, "dp", [(i, i ^ flip) for i in range(4)])
        found.append(piece)
    return found


def tail_twice(values):
    return jnp.concatenate([values, values[:, LANES:]], axis=1)


def pair_kernel(got_ref, hidden_ref, first_ref, second_ref, cotangent_ref, *outs):
    back_ref, part_ref, feature_ref, delta_ref = outs
    chan_count = hidden_ref.shape[1]
    slots = got_ref.shape[0]
    note = got_ref[:, chan_count:].astype(jnp.float32)
    score = note[:, 1:2] + note[:, 2:3] + note[:, 3:4]
    row_ids = lax.broadcasted_iota(jnp.int32, (slots, hidden_ref.shape[0]), 1).astype(jnp.float32)
    hits = (note[:, 0:1] == row_ids).astype(jnp.float32).astype(jnp.bfloat16)
    accept = jnp.dot(hits, hidden_ref[...], preferred_element_type=jnp.float32)
    donor = got_ref[:, :chan_count].astype(jnp.float32)
    feature = (donor * accept).astype(jnp.bfloat16)
    feature_ref[...] = feature
    head_preact = jnp.dot(feature, first_ref[...], preferred_element_type=jnp.float32)
    delta = (score * second_ref[...].astype(jnp.float32) * gelu_slope(head_preact)).astype(
        jnp.bfloat16
    )
    delta_ref[...] = delta
    feature_grad = lax.dot_general(
        delta, first_ref[...], (((1,), (1,)), ((), ())), preferred_element_type=jnp.float32
    )
    back_ref[...] = (feature_grad * accept).astype(jnp.bfloat16)
    accept_grad = (feature_grad * donor).astype(jnp.bfloat16)
    part_ref[...] = cotangent_ref[...].astype(jnp.float32) + contract_rows(hits, accept_grad)


def head_kernel(scale, *refs):
    term = contract_rows(refs[4][...], refs[0][...])
    for feature, delta in zip(refs[1:4], refs[5:8], strict=True):
        term = term + contract_rows(delta[...], feature[...])
    refs[8][...] = (term.T * scale).astype(jnp.bfloat16)


def weight_kernel(scale, taps, grid, *refs):
    normed_ref, head_ref, grads, out_ref, tail_ref = refs[0], refs[1], refs[2:6], refs[6], refs[7]
    ys, zs, xs = grid
    chan_count = normed_ref.shape[0]
    width = 2 * LANES
    reach = (taps - 1) * DILATION
    share = tail_ref.shape[0] // (ys * zs * xs)
    chunk = share * zs + share * zs // 2
    values = [tail_twice(ref[...].astype(jnp.float32)) for ref in grads]

    def put(first, block):
        tail_ref[first : first + block.shape[0], :] = block[:, LANES:]
        done = 0
        while done < block.shape[0]:
            owner, inside = divmod(first + done, share)
            step = min(share - inside, block.shape[0] - done)
            y, z, x = owner // (zs * xs), owner // xs % zs, owner % xs
            start = (y * xs + x) * chunk + z * share + inside
            out_ref[start : start + step, :] = block[done : done + step, :LANES].astype(jnp.bfloat16)
            done += step

    for k in range(taps):
        pieces = []
        for value in values:
            if k:
                pieces.append(jnp.zeros((k * DILATION, width), jnp.float32))
            pieces.append(value)
            if k < taps - 1:
                pieces.append(jnp.zeros((reach - k * DILATION, width), jnp.float32))
        shifted = jnp.concatenate(pieces, axis=0).astype(jnp.bfloat16)
        put(
            k * chan_count,
            jnp.dot(normed_ref[...], shifted, preferred_element_type=jnp.float32) * scale,
        )
    put(taps * chan_count, tail_twice(head_ref[...].astype(jnp.float32)))
    low = lax.broadcasted_iota(jnp.int32, (share, LANES), 1) < LANES // 2
    for y in range(ys):
        for x in range(xs):
            for z in range(zs // 2):
                rows = [((y * zs + half) * xs + x) * share for half in (z, z + zs // 2)]
                start = (y * xs + x) * chunk + (zs + z) * share
                out_ref[start : start + share, :] = jnp.where(
                    low, tail_ref[rows[0] : rows[0] + share, :], tail_ref[rows[1] : rows[1] + share, :]
                ).astype(jnp.bfloat16)


def fold_kernel(share, zs, terms_ref, out_ref):
    total = terms_ref[0].astype(jnp.float32)
    for index in range(1, terms_ref.shape[0]):
        total = total + terms_ref[index].astype(jnp.float32)
    for z in range(zs):
        out_ref[z, :share, :] = total[z * share : (z + 1) * share].astype(jnp.bfloat16)
        first = (zs + z % (zs // 2)) * share
        out_ref[z, share:, :] = total[first : first + share].astype(jnp.bfloat16)


def in_vmem(kernel, shapes, count, limit, scratch=()):
    spec = pl.BlockSpec(memory_space=pltpu.VMEM)
    return pl.pallas_call(
        kernel,
        out_shape=shapes,
        in_specs=[spec] * count,
        out_specs=jax.tree.map(lambda _: spec, shapes),
        scratch_shapes=scratch,
        compiler_params=pltpu.CompilerParams(vmem_limit_bytes=limit),
    )


def per_device(
    activations,
    conv_weight,
    head_first,
    head_second,
    hidden_cotangent,
    score_cotangent,
    donor_row,
    acceptor_owner,
    acceptor_row,
):
    row_count = activations.shape[1]
    chan_count = activations.shape[2]
    out_count = conv_weight.shape[1]
    tap_count = conv_weight.shape[0] // chan_count
    reach_rows = (tap_count - 1) // 2 * DILATION
    shards = lax.axis_size("seq")
    dp_count = lax.axis_size("dp")
    pair_count = donor_row.shape[1]
    capacity = max(2, 2 * pair_count // shards)
    slots = shards * capacity
    col_width = out_count // dp_count

    above, below = seq_halo(activations[0], reach_rows)
    owner = acceptor_owner[0, :, 0]
    pair_ids = jnp.arange(pair_count, dtype=jnp.int32)
    rank = jnp.sum(
        ((owner[:, None] == owner[None, :]) & (pair_ids[None, :] < pair_ids[:, None])).astype(
            jnp.int32
        ),
        axis=1,
    )
    target = owner * capacity + rank
    placed = target[None, :] == jnp.arange(slots, dtype=jnp.int32)[:, None]
    score = score_cotangent[0]
    high = lax.reduce_precision(score, 8, 7)
    middle = lax.reduce_precision(score - high, 8, 7)
    note = jnp.stack([acceptor_row[0].astype(jnp.float32) + 1.0, high, middle, score - high - middle])
    note = jnp.pad(note, ((0, LANES - note.shape[0]), (0, 0))).astype(jnp.bfloat16)
    notes = lax.dot_general(
        placed.astype(jnp.bfloat16), note, (((1,), (1,)), ((), ())), preferred_element_type=jnp.float32
    )
    notes = (notes - (jnp.arange(LANES) == 0).astype(jnp.float32)[None, :]).astype(jnp.bfloat16)
    donor_slot = (
        jnp.sum(jnp.where(placed, donor_row[0][None, :] + 1, 0), axis=1, dtype=jnp.int32) - 1
    )
    row_ids = jnp.arange(row_count, dtype=jnp.int32)
    hits = (donor_slot[:, None] == row_ids[None, :]).astype(jnp.bfloat16)
    hits, notes = lax.optimization_barrier((hits, notes))

    padded_input = jnp.concatenate([above, activations[0], below], axis=0)
    core_input, z_input = swap_core(padded_input), swap_z(padded_input)
    padded_peers = padded_input, core_input, z_input, swap_core(z_input)

    def normalise(field):
        values = field.astype(jnp.float32)
        inverse = lax.rsqrt(jnp.mean(values * values, axis=1, keepdims=True) + 1e-05)
        return values, inverse, (values * inverse).astype(jnp.bfloat16)

    _, padded_inverse, padded = normalise(padded_input)
    norm_inverse = padded_inverse[reach_rows : reach_rows + row_count]

    def tap_columns(field):
        return jnp.concatenate(
            [field[k * DILATION : k * DILATION + row_count] for k in range(tap_count)], axis=1
        )

    columns = tap_columns(padded)
    preact = jnp.dot(columns, conv_weight, preferred_element_type=jnp.float32)
    hidden = jax.nn.gelu(preact, approximate=False).astype(jnp.bfloat16)
    slope = gelu_slope(preact)
    hidden, slope = lax.optimization_barrier((hidden, slope))

    sent = jnp.concatenate(
        [jnp.dot(hits, hidden, preferred_element_type=jnp.float32).astype(jnp.bfloat16), notes], axis=1
    )
    got = lax.all_to_all(
        sent.reshape(shards, capacity, out_count + LANES),
        "seq",
        split_axis=0,
        concat_axis=0,
        tiled=True,
    ).reshape(slots, out_count + LANES)
    slot_shape = jax.ShapeDtypeStruct((slots, out_count), jnp.bfloat16)
    back, part, feature, delta = in_vmem(
        pair_kernel,
        (
            slot_shape,
            jax.ShapeDtypeStruct((row_count, out_count), jnp.float32),
            slot_shape,
            slot_shape,
        ),
        5,
        KERNEL_VMEM,
    )(got, hidden, head_first, head_second.reshape(1, out_count), hidden_cotangent[0])
    donor_grad = lax.all_to_all(
        back.reshape(shards, capacity, out_count),
        "seq",
        split_axis=0,
        concat_axis=0,
        tiled=True,
    ).reshape(slots, out_count)
    feature_peers = dp_peers(feature)
    delta_peers = dp_columns(delta, col_width)
    head_term = in_vmem(
        functools.partial(head_kernel, 1.0 / math.sqrt(dp_count * pair_count * shards)),
        jax.ShapeDtypeStruct((out_count, col_width), jnp.bfloat16),
        8,
        KERNEL_VMEM,
    )(*feature_peers, *delta_peers)
    hidden_grad = part + contract_rows(hits, donor_grad)
    preact_grad = (hidden_grad * slope).astype(jnp.bfloat16)
    grad_peers = dp_columns(preact_grad, col_width)

    normed_all = jnp.concatenate(
        [padded] + [normalise(peer)[2] for peer in padded_peers[1:]], axis=0
    ).T
    ys, zs, xs = SEQ_GRID
    row_total = tap_count * chan_count + out_count
    share = row_total // shards
    chunk = share * zs + share * zs // 2
    term = in_vmem(
        functools.partial(
            weight_kernel, 1.0 / math.sqrt(dp_count * row_count * shards), tap_count, SEQ_GRID
        ),
        jax.ShapeDtypeStruct((ys * xs * chunk, LANES), jnp.bfloat16),
        6,
        KERNEL_VMEM,
        [pltpu.VMEM((row_total, LANES), jnp.float32)],
    )(normed_all, head_term, *grad_peers)
    term, halo_source = lax.optimization_barrier((term, preact_grad))
    terms = lax.all_to_all(
        term.reshape(ys * xs, chunk, LANES),
        "seq",
        split_axis=0,
        concat_axis=0,
        tiled=True,
        axis_index_groups=[
            [(y * zs + z) * xs + x for y in range(ys) for x in range(xs)] for z in range(zs)
        ],
    )
    folded = in_vmem(
        functools.partial(fold_kernel, share, zs),
        jax.ShapeDtypeStruct((zs, 2 * share, LANES), jnp.bfloat16),
        1,
        KERNEL_VMEM,
    )(terms)
    shares = lax.all_to_all(
        folded,
        "seq",
        split_axis=0,
        concat_axis=0,
        tiled=True,
        axis_index_groups=[
            [(y * zs + z) * xs + x for z in range(zs)] for y in range(ys) for x in range(xs)
        ],
    )
    total = jnp.sum(shares.astype(jnp.float32), axis=0)
    upper = lax.axis_index("seq") // xs % zs >= zs // 2
    others = jnp.where(upper, total[share:, LANES // 2 :], total[share:, : LANES // 2])
    weight_grads = jnp.concatenate([total[:share], others], axis=1)

    input_grad = data_grad(
        activations[0], norm_inverse, halo_source, conv_weight, reach_rows, tap_count
    )
    return (input_grad.astype(jnp.bfloat16)[None], weight_grads)


def data_grad(inputs, norm_inverse, preact_grad, conv_weight, reach_rows, tap_count):
    row_count, chan_count = inputs.shape
    input_values = inputs.astype(jnp.float32)
    grad_above, grad_below = seq_halo(preact_grad, reach_rows)
    grad_padded = jnp.concatenate([grad_above, preact_grad, grad_below], axis=0)
    spread = lax.dot_general(
        grad_padded, conv_weight, (((1,), (1,)), ((), ())), preferred_element_type=jnp.float32
    )
    normed_grad = spread[2 * reach_rows : 2 * reach_rows + row_count, 0:chan_count]
    for tap_index in range(1, tap_count):
        first_row = 2 * reach_rows - tap_index * DILATION
        normed_grad = (
            normed_grad
            + spread[
                first_row : first_row + row_count,
                tap_index * chan_count : (tap_index + 1) * chan_count,
            ]
        )
    return norm_inverse * normed_grad - input_values * norm_inverse**3 * jnp.mean(
        normed_grad * input_values, axis=1, keepdims=True
    )


def solution(mesh):
    placed = (
        P("dp", "seq", None),
        P(),
        P(),
        P(),
        P("dp", "seq", None),
        P("dp", "seq"),
        P("dp", "seq"),
        P("dp", "seq", None),
        P("dp", "seq"),
    )

    return jax.shard_map(
        per_device,
        mesh=mesh,
        in_specs=placed,
        out_specs=(P("dp", "seq", None), P("seq", "dp")),
        check_vma=False,
    )
```

```python
import functools
import math

import jax
import jax.numpy as jnp
from jax import lax
from jax.experimental import pallas as pl
from jax.experimental.pallas import tpu as pltpu
from jax.sharding import PartitionSpec as P


DILATION = 8
LANES = 128
SEQ_GRID = (4, 4, 4)
KERNEL_VMEM = 16 * 1024 * 1024


def gelu_slope(values):
    normal_cdf = 0.5 * (1.0 + lax.erf(values * (1.0 / math.sqrt(2.0))))
    density = jnp.exp(-0.5 * values * values) * (1.0 / math.sqrt(2.0 * math.pi))
    return normal_cdf + values * density


def contract_rows(left_side, right_side):
    return lax.dot_general(
        left_side, right_side, (((0,), (0,)), ((), ())), preferred_element_type=jnp.float32
    )


def seq_halo(cells, width):
    count = lax.axis_size("seq")
    above = lax.ppermute(cells[-width:], "seq", [(i, i + 1) for i in range(count - 1)])
    below = lax.ppermute(cells[:width], "seq", [(i + 1, i) for i in range(count - 1)])
    return above, below


def swap_core(field):
    return lax.ppermute(field, "dp", [(0, 1), (1, 0), (2, 3), (3, 2)])


def swap_z(field):
    return lax.ppermute(field, "dp", [(0, 2), (1, 3), (2, 0), (3, 1)])


def dp_peers(field):
    core = swap_core(field)
    z_side = swap_z(field)
    return field, core, z_side, swap_core(z_side)


def dp_columns(field, width):
    index = lax.axis_index("dp")
    found = []
    for flip in range(4):
        piece = lax.dynamic_slice_in_dim(field, (index ^ flip) * width, width, axis=1)
        if flip:
            piece = lax.ppermute(piece, "dp", [(i, i ^ flip) for i in range(4)])
        found.append(piece)
    return found


def tail_twice(values):
    return jnp.concatenate([values, values[:, LANES:]], axis=1)


def conv_kernel(taps, above_ref, input_ref, below_ref, hits_ref, notes_ref, weight_ref, *rest):
    padded_ref, hidden_ref, slope_ref, sent_ref, held_ref, done = rest
    row_count, chan_count = input_ref.shape
    copies = []
    for k in range(taps):
        rows = pl.ds(k * chan_count, chan_count)
        copies.append(pltpu.make_async_copy(weight_ref.at[rows], held_ref.at[rows], done.at[k]))
        copies[-1].start()
    values = jnp.concatenate([above_ref[...], input_ref[...], below_ref[...]], axis=0).astype(
        jnp.float32
    )
    inverse = lax.rsqrt(jnp.mean(values * values, axis=1, keepdims=True) + 1e-05)
    normed = values * inverse
    padded_ref[...] = normed.astype(jnp.bfloat16)
    preact = jnp.zeros((row_count, hidden_ref.shape[1]), jnp.float32)
    for k in range(taps):
        column = normed[k * DILATION : k * DILATION + row_count].astype(jnp.bfloat16)
        copies[k].wait()
        preact = preact + jnp.dot(
            column,
            held_ref[k * chan_count : (k + 1) * chan_count, :],
            preferred_element_type=jnp.float32,
        )
    normal_cdf = 0.5 * (1.0 + lax.erf(preact * (1.0 / math.sqrt(2.0))))
    density = jnp.exp(-0.5 * preact * preact) * (1.0 / math.sqrt(2.0 * math.pi))
    hidden = (preact * normal_cdf).astype(jnp.bfloat16)
    hidden_ref[...] = hidden
    slope_ref[...] = normal_cdf + preact * density
    out_count = hidden_ref.shape[1]
    sent_ref[:, :out_count] = jnp.dot(
        hits_ref[...], hidden, preferred_element_type=jnp.float32
    ).astype(jnp.bfloat16)
    sent_ref[:, out_count:] = notes_ref[...]


def pair_kernel(got_ref, hidden_ref, first_ref, second_ref, cotangent_ref, *outs):
    back_ref, part_ref, feature_ref, delta_ref = outs
    chan_count = hidden_ref.shape[1]
    slots = got_ref.shape[0]
    note = got_ref[:, chan_count:].astype(jnp.float32)
    score = note[:, 1:2] + note[:, 2:3] + note[:, 3:4]
    row_ids = lax.broadcasted_iota(jnp.int32, (slots, hidden_ref.shape[0]), 1).astype(jnp.float32)
    hits = (note[:, 0:1] == row_ids).astype(jnp.float32).astype(jnp.bfloat16)
    accept = jnp.dot(hits, hidden_ref[...], preferred_element_type=jnp.float32)
    donor = got_ref[:, :chan_count].astype(jnp.float32)
    feature = (donor * accept).astype(jnp.bfloat16)
    feature_ref[...] = feature
    head_preact = jnp.dot(feature, first_ref[...], preferred_element_type=jnp.float32)
    delta = (score * second_ref[...].astype(jnp.float32) * gelu_slope(head_preact)).astype(
        jnp.bfloat16
    )
    delta_ref[...] = delta
    feature_grad = lax.dot_general(
        delta, first_ref[...], (((1,), (1,)), ((), ())), preferred_element_type=jnp.float32
    )
    back_ref[...] = (feature_grad * accept).astype(jnp.bfloat16)
    accept_grad = (feature_grad * donor).astype(jnp.bfloat16)
    part_ref[...] = cotangent_ref[...].astype(jnp.float32) + contract_rows(hits, accept_grad)


def head_kernel(scale, *refs):
    term = contract_rows(refs[4][...], refs[0][...])
    for feature, delta in zip(refs[1:4], refs[5:8], strict=True):
        term = term + contract_rows(delta[...], feature[...])
    refs[8][...] = (term.T * scale).astype(jnp.bfloat16)


def weight_kernel(scale, taps, grid, *refs):
    normed_ref, head_ref, grads, out_ref, tail_ref = refs[0], refs[1], refs[2:6], refs[6], refs[7]
    ys, zs, xs = grid
    chan_count = normed_ref.shape[0]
    width = 2 * LANES
    reach = (taps - 1) * DILATION
    share = tail_ref.shape[0] // (ys * zs * xs)
    chunk = share * zs + share * zs // 2
    values = [tail_twice(ref[...].astype(jnp.float32)) for ref in grads]

    def put(first, block):
        tail_ref[first : first + block.shape[0], :] = block[:, LANES:]
        done = 0
        while done < block.shape[0]:
            owner, inside = divmod(first + done, share)
            step = min(share - inside, block.shape[0] - done)
            y, z, x = owner // (zs * xs), owner // xs % zs, owner % xs
            start = (y * xs + x) * chunk + z * share + inside
            out_ref[start : start + step, :] = block[done : done + step, :LANES].astype(jnp.bfloat16)
            done += step

    for k in range(taps):
        pieces = []
        for value in values:
            if k:
                pieces.append(jnp.zeros((k * DILATION, width), jnp.float32))
            pieces.append(value)
            if k < taps - 1:
                pieces.append(jnp.zeros((reach - k * DILATION, width), jnp.float32))
        shifted = jnp.concatenate(pieces, axis=0).astype(jnp.bfloat16)
        put(
            k * chan_count,
            jnp.dot(normed_ref[...], shifted, preferred_element_type=jnp.float32) * scale,
        )
    put(taps * chan_count, tail_twice(head_ref[...].astype(jnp.float32)))
    low = lax.broadcasted_iota(jnp.int32, (share, LANES), 1) < LANES // 2
    for y in range(ys):
        for x in range(xs):
            for z in range(zs // 2):
                rows = [((y * zs + half) * xs + x) * share for half in (z, z + zs // 2)]
                start = (y * xs + x) * chunk + (zs + z) * share
                out_ref[start : start + share, :] = jnp.where(
                    low, tail_ref[rows[0] : rows[0] + share, :], tail_ref[rows[1] : rows[1] + share, :]
                ).astype(jnp.bfloat16)


def fold_kernel(share, zs, terms_ref, out_ref):
    total = terms_ref[0].astype(jnp.float32)
    for index in range(1, terms_ref.shape[0]):
        total = total + terms_ref[index].astype(jnp.float32)
    for z in range(zs):
        out_ref[z, :share, :] = total[z * share : (z + 1) * share].astype(jnp.bfloat16)
        first = (zs + z % (zs // 2)) * share
        out_ref[z, share:, :] = total[first : first + share].astype(jnp.bfloat16)


def in_vmem(kernel, shapes, count, limit, scratch=()):
    spec = pl.BlockSpec(memory_space=pltpu.VMEM)
    return pl.pallas_call(
        kernel,
        out_shape=shapes,
        in_specs=[spec] * count,
        out_specs=jax.tree.map(lambda _: spec, shapes),
        scratch_shapes=scratch,
        compiler_params=pltpu.CompilerParams(vmem_limit_bytes=limit),
    )


def per_device(
    activations,
    conv_weight,
    head_first,
    head_second,
    hidden_cotangent,
    score_cotangent,
    donor_row,
    acceptor_owner,
    acceptor_row,
):
    row_count = activations.shape[1]
    chan_count = activations.shape[2]
    out_count = conv_weight.shape[1]
    tap_count = conv_weight.shape[0] // chan_count
    reach_rows = (tap_count - 1) // 2 * DILATION
    shards = lax.axis_size("seq")
    dp_count = lax.axis_size("dp")
    pair_count = donor_row.shape[1]
    capacity = max(2, 2 * pair_count // shards)
    slots = shards * capacity
    col_width = out_count // dp_count

    above, below = seq_halo(activations[0], reach_rows)
    owner = acceptor_owner[0, :, 0]
    pair_ids = jnp.arange(pair_count, dtype=jnp.int32)
    rank = jnp.sum(
        ((owner[:, None] == owner[None, :]) & (pair_ids[None, :] < pair_ids[:, None])).astype(
            jnp.int32
        ),
        axis=1,
    )
    target = owner * capacity + rank
    placed = target[None, :] == jnp.arange(slots, dtype=jnp.int32)[:, None]
    score = score_cotangent[0]
    high = lax.reduce_precision(score, 8, 7)
    middle = lax.reduce_precision(score - high, 8, 7)
    note = jnp.stack([acceptor_row[0].astype(jnp.float32) + 1.0, high, middle, score - high - middle])
    note = jnp.pad(note, ((0, LANES - note.shape[0]), (0, 0))).astype(jnp.bfloat16)
    notes = lax.dot_general(
        placed.astype(jnp.bfloat16), note, (((1,), (1,)), ((), ())), preferred_element_type=jnp.float32
    )
    notes = (notes - (jnp.arange(LANES) == 0).astype(jnp.float32)[None, :]).astype(jnp.bfloat16)
    donor_slot = (
        jnp.sum(jnp.where(placed, donor_row[0][None, :] + 1, 0), axis=1, dtype=jnp.int32) - 1
    )
    row_ids = jnp.arange(row_count, dtype=jnp.int32)
    hits = (donor_slot[:, None] == row_ids[None, :]).astype(jnp.bfloat16)
    hits, notes = lax.optimization_barrier((hits, notes))

    padded_input = jnp.concatenate([above, activations[0], below], axis=0)
    core_input, z_input = swap_core(padded_input), swap_z(padded_input)
    padded_peers = padded_input, core_input, z_input, swap_core(z_input)

    def normalise(field):
        values = field.astype(jnp.float32)
        inverse = lax.rsqrt(jnp.mean(values * values, axis=1, keepdims=True) + 1e-05)
        return (values * inverse).astype(jnp.bfloat16)

    spec = pl.BlockSpec(memory_space=pltpu.VMEM)
    padded, hidden, slope, sent = pl.pallas_call(
        functools.partial(conv_kernel, tap_count),
        out_shape=(
            jax.ShapeDtypeStruct((row_count + 2 * reach_rows, chan_count), jnp.bfloat16),
            jax.ShapeDtypeStruct((row_count, out_count), jnp.bfloat16),
            jax.ShapeDtypeStruct((row_count, out_count), jnp.float32),
            jax.ShapeDtypeStruct((slots, out_count + LANES), jnp.bfloat16),
        ),
        in_specs=[spec] * 5 + [pl.BlockSpec(memory_space=pl.ANY)],
        out_specs=(spec,) * 4,
        scratch_shapes=[
            pltpu.VMEM(conv_weight.shape, jnp.bfloat16),
            pltpu.SemaphoreType.DMA((tap_count,)),
        ],
        compiler_params=pltpu.CompilerParams(vmem_limit_bytes=KERNEL_VMEM),
    )(above, activations[0], below, hits, notes, conv_weight)
    got = lax.all_to_all(
        sent.reshape(shards, capacity, out_count + LANES),
        "seq",
        split_axis=0,
        concat_axis=0,
        tiled=True,
    ).reshape(slots, out_count + LANES)
    slot_shape = jax.ShapeDtypeStruct((slots, out_count), jnp.bfloat16)
    back, part, feature, delta = in_vmem(
        pair_kernel,
        (
            slot_shape,
            jax.ShapeDtypeStruct((row_count, out_count), jnp.float32),
            slot_shape,
            slot_shape,
        ),
        5,
        KERNEL_VMEM,
    )(got, hidden, head_first, head_second.reshape(1, out_count), hidden_cotangent[0])
    donor_grad = lax.all_to_all(
        back.reshape(shards, capacity, out_count),
        "seq",
        split_axis=0,
        concat_axis=0,
        tiled=True,
    ).reshape(slots, out_count)
    feature_peers = dp_peers(feature)
    delta_peers = dp_columns(delta, col_width)
    head_term = in_vmem(
        functools.partial(head_kernel, 1.0 / math.sqrt(dp_count * pair_count * shards)),
        jax.ShapeDtypeStruct((out_count, col_width), jnp.bfloat16),
        8,
        KERNEL_VMEM,
    )(*feature_peers, *delta_peers)
    hidden_grad = part + contract_rows(hits, donor_grad)
    preact_grad = (hidden_grad * slope).astype(jnp.bfloat16)
    grad_peers = dp_columns(preact_grad, col_width)
    grad_above, grad_below = seq_halo(preact_grad, reach_rows)

    normed_all = jnp.concatenate(
        [padded] + [normalise(peer) for peer in padded_peers[1:]], axis=0
    ).T
    ys, zs, xs = SEQ_GRID
    row_total = tap_count * chan_count + out_count
    share = row_total // shards
    chunk = share * zs + share * zs // 2
    term = in_vmem(
        functools.partial(
            weight_kernel, 1.0 / math.sqrt(dp_count * row_count * shards), tap_count, SEQ_GRID
        ),
        jax.ShapeDtypeStruct((ys * xs * chunk, LANES), jnp.bfloat16),
        6,
        KERNEL_VMEM,
        [pltpu.VMEM((row_total, LANES), jnp.float32)],
    )(normed_all, head_term, *grad_peers)
    terms = lax.all_to_all(
        term.reshape(ys * xs, chunk, LANES),
        "seq",
        split_axis=0,
        concat_axis=0,
        tiled=True,
        axis_index_groups=[
            [(y * zs + z) * xs + x for y in range(ys) for x in range(xs)] for z in range(zs)
        ],
    )
    folded = in_vmem(
        functools.partial(fold_kernel, share, zs),
        jax.ShapeDtypeStruct((zs, 2 * share, LANES), jnp.bfloat16),
        1,
        KERNEL_VMEM,
    )(terms)
    shares = lax.all_to_all(
        folded,
        "seq",
        split_axis=0,
        concat_axis=0,
        tiled=True,
        axis_index_groups=[
            [(y * zs + z) * xs + x for z in range(zs)] for y in range(ys) for x in range(xs)
        ],
    )
    total = jnp.sum(shares.astype(jnp.float32), axis=0)
    upper = lax.axis_index("seq") // xs % zs >= zs // 2
    others = jnp.where(upper, total[share:, LANES // 2 :], total[share:, : LANES // 2])
    weight_grads = jnp.concatenate([total[:share], others], axis=1)

    input_grad = data_grad(
        activations[0], grad_above, preact_grad, grad_below, conv_weight, tap_count
    )
    return (input_grad.astype(jnp.bfloat16)[None], weight_grads)


def data_grad(inputs, grad_above, preact_grad, grad_below, conv_weight, tap_count):
    reach_rows = grad_above.shape[0]
    row_count, chan_count = inputs.shape
    input_values = inputs.astype(jnp.float32)
    norm_inverse = lax.rsqrt(
        jnp.mean(input_values * input_values, axis=1, keepdims=True) + 1e-05
    )
    grad_padded = jnp.concatenate([grad_above, preact_grad, grad_below], axis=0)
    spread = lax.dot_general(
        grad_padded, conv_weight, (((1,), (1,)), ((), ())), preferred_element_type=jnp.float32
    )
    normed_grad = spread[2 * reach_rows : 2 * reach_rows + row_count, 0:chan_count]
    for tap_index in range(1, tap_count):
        first_row = 2 * reach_rows - tap_index * DILATION
        normed_grad = (
            normed_grad
            + spread[
                first_row : first_row + row_count,
                tap_index * chan_count : (tap_index + 1) * chan_count,
            ]
        )
    return norm_inverse * normed_grad - input_values * norm_inverse**3 * jnp.mean(
        normed_grad * input_values, axis=1, keepdims=True
    )


def solution(mesh):
    placed = (
        P("dp", "seq", None),
        P(),
        P(),
        P(),
        P("dp", "seq", None),
        P("dp", "seq"),
        P("dp", "seq"),
        P("dp", "seq", None),
        P("dp", "seq"),
    )

    return jax.shard_map(
        per_device,
        mesh=mesh,
        in_specs=placed,
        out_specs=(P("dp", "seq", None), P("seq", "dp")),
        check_vma=False,
    )
```

```python
import functools
import math

import jax
import jax.numpy as jnp
from jax import lax
from jax.experimental import pallas as pl
from jax.experimental.pallas import tpu as pltpu
from jax.sharding import PartitionSpec as P


DILATION = 8
LANES = 128
SEQ_GRID = (4, 4, 4)
KERNEL_VMEM = 16 * 1024 * 1024


def gelu_slope(values):
    normal_cdf = 0.5 * (1.0 + lax.erf(values * (1.0 / math.sqrt(2.0))))
    density = jnp.exp(-0.5 * values * values) * (1.0 / math.sqrt(2.0 * math.pi))
    return normal_cdf + values * density


def contract_rows(left_side, right_side):
    return lax.dot_general(
        left_side, right_side, (((0,), (0,)), ((), ())), preferred_element_type=jnp.float32
    )


def seq_halo(cells, width):
    count = lax.axis_size("seq")
    above = lax.ppermute(cells[-width:], "seq", [(i, i + 1) for i in range(count - 1)])
    below = lax.ppermute(cells[:width], "seq", [(i + 1, i) for i in range(count - 1)])
    return above, below


def swap_core(field):
    return lax.ppermute(field, "dp", [(0, 1), (1, 0), (2, 3), (3, 2)])


def swap_z(field):
    return lax.ppermute(field, "dp", [(0, 2), (1, 3), (2, 0), (3, 1)])


def dp_peers(field):
    core = swap_core(field)
    z_side = swap_z(field)
    return field, core, z_side, swap_core(z_side)


def dp_columns(field, width):
    index = lax.axis_index("dp")
    found = []
    for flip in range(4):
        piece = lax.dynamic_slice_in_dim(field, (index ^ flip) * width, width, axis=1)
        if flip:
            piece = lax.ppermute(piece, "dp", [(i, i ^ flip) for i in range(4)])
        found.append(piece)
    return found


def tail_twice(values):
    return jnp.concatenate([values, values[:, LANES:]], axis=1)


def conv_kernel(taps, above_ref, input_ref, below_ref, hits_ref, notes_ref, weight_ref, *rest):
    padded_out, hidden_out, slope_out, sent_ref, held_ref, padded_ref, hidden_ref, slope_ref, done = rest
    row_count, chan_count = input_ref.shape
    leaving = [
        pltpu.make_async_copy(source, target, done.at[taps + index])
        for index, (source, target) in enumerate(
            ((padded_ref, padded_out), (hidden_ref, hidden_out), (slope_ref, slope_out))
        )
    ]
    copies = []
    for k in range(taps):
        rows = pl.ds(k * chan_count, chan_count)
        copies.append(pltpu.make_async_copy(weight_ref.at[rows], held_ref.at[rows], done.at[k]))
        copies[-1].start()
    values = jnp.concatenate([above_ref[...], input_ref[...], below_ref[...]], axis=0).astype(
        jnp.float32
    )
    inverse = lax.rsqrt(jnp.mean(values * values, axis=1, keepdims=True) + 1e-05)
    normed = values * inverse
    padded_ref[...] = normed.astype(jnp.bfloat16)
    leaving[0].start()
    preact = jnp.zeros((row_count, hidden_ref.shape[1]), jnp.float32)
    for k in range(taps):
        column = normed[k * DILATION : k * DILATION + row_count].astype(jnp.bfloat16)
        copies[k].wait()
        preact = preact + jnp.dot(
            column,
            held_ref[k * chan_count : (k + 1) * chan_count, :],
            preferred_element_type=jnp.float32,
        )
    normal_cdf = 0.5 * (1.0 + lax.erf(preact * (1.0 / math.sqrt(2.0))))
    density = jnp.exp(-0.5 * preact * preact) * (1.0 / math.sqrt(2.0 * math.pi))
    hidden = (preact * normal_cdf).astype(jnp.bfloat16)
    hidden_ref[...] = hidden
    leaving[1].start()
    slope_ref[...] = normal_cdf + preact * density
    leaving[2].start()
    out_count = hidden_ref.shape[1]
    sent_ref[:, :out_count] = jnp.dot(
        hits_ref[...], hidden, preferred_element_type=jnp.float32
    ).astype(jnp.bfloat16)
    sent_ref[:, out_count:] = notes_ref[...]
    for copy in leaving:
        copy.wait()


def turn_kernel(own_ref, *refs):
    peers, out_ref = refs[:-1], refs[-1]
    pieces = [own_ref[...].astype(jnp.float32)]
    for peer in peers:
        values = peer[...].astype(jnp.float32)
        inverse = lax.rsqrt(jnp.mean(values * values, axis=1, keepdims=True) + 1e-05)
        pieces.append(values * inverse)
    out_ref[...] = jnp.concatenate(pieces, axis=0).T.astype(jnp.bfloat16)


def pair_kernel(got_ref, hidden_in, first_ref, second_ref, cotangent_ref, *rest):
    back_ref, part_out, feature_ref, delta_ref, hidden_ref, part_ref, done = rest
    hidden_copy = pltpu.make_async_copy(hidden_in, hidden_ref, done.at[0])
    part_copy = pltpu.make_async_copy(part_ref, part_out, done.at[1])
    hidden_copy.start()
    chan_count = hidden_ref.shape[1]
    slots = got_ref.shape[0]
    note = got_ref[:, chan_count:].astype(jnp.float32)
    score = note[:, 1:2] + note[:, 2:3] + note[:, 3:4]
    row_ids = lax.broadcasted_iota(jnp.int32, (slots, hidden_ref.shape[0]), 1).astype(jnp.float32)
    hits = (note[:, 0:1] == row_ids).astype(jnp.float32).astype(jnp.bfloat16)
    hidden_copy.wait()
    accept = jnp.dot(hits, hidden_ref[...], preferred_element_type=jnp.float32)
    donor = got_ref[:, :chan_count].astype(jnp.float32)
    feature = (donor * accept).astype(jnp.bfloat16)
    feature_ref[...] = feature
    head_preact = jnp.dot(feature, first_ref[...], preferred_element_type=jnp.float32)
    delta = (score * second_ref[...].astype(jnp.float32) * gelu_slope(head_preact)).astype(
        jnp.bfloat16
    )
    delta_ref[...] = delta
    feature_grad = lax.dot_general(
        delta, first_ref[...], (((1,), (1,)), ((), ())), preferred_element_type=jnp.float32
    )
    accept_grad = (feature_grad * donor).astype(jnp.bfloat16)
    part_ref[...] = cotangent_ref[...].astype(jnp.float32) + contract_rows(hits, accept_grad)
    part_copy.start()
    back_ref[...] = (feature_grad * accept).astype(jnp.bfloat16)
    part_copy.wait()


def head_kernel(scale, *refs):
    term = contract_rows(refs[4][...], refs[0][...])
    for feature, delta in zip(refs[1:4], refs[5:8], strict=True):
        term = term + contract_rows(delta[...], feature[...])
    refs[8][...] = (term.T * scale).astype(jnp.bfloat16)


def weight_kernel(scale, taps, grid, *refs):
    normed_ref, head_ref, grads, out_ref, tail_ref = refs[0], refs[1], refs[2:6], refs[6], refs[7]
    ys, zs, xs = grid
    chan_count = normed_ref.shape[0]
    width = 2 * LANES
    reach = (taps - 1) * DILATION
    share = tail_ref.shape[0] // (ys * zs * xs)
    chunk = share * zs + share * zs // 2
    values = [tail_twice(ref[...].astype(jnp.float32)) for ref in grads]

    def put(first, block):
        tail_ref[first : first + block.shape[0], :] = block[:, LANES:]
        done = 0
        while done < block.shape[0]:
            owner, inside = divmod(first + done, share)
            step = min(share - inside, block.shape[0] - done)
            y, z, x = owner // (zs * xs), owner // xs % zs, owner % xs
            start = (y * xs + x) * chunk + z * share + inside
            out_ref[start : start + step, :] = block[done : done + step, :LANES].astype(jnp.bfloat16)
            done += step

    for k in range(taps):
        pieces = []
        for value in values:
            if k:
                pieces.append(jnp.zeros((k * DILATION, width), jnp.float32))
            pieces.append(value)
            if k < taps - 1:
                pieces.append(jnp.zeros((reach - k * DILATION, width), jnp.float32))
        shifted = jnp.concatenate(pieces, axis=0).astype(jnp.bfloat16)
        put(
            k * chan_count,
            jnp.dot(normed_ref[...], shifted, preferred_element_type=jnp.float32) * scale,
        )
    put(taps * chan_count, tail_twice(head_ref[...].astype(jnp.float32)))
    low = lax.broadcasted_iota(jnp.int32, (share, LANES), 1) < LANES // 2
    for y in range(ys):
        for x in range(xs):
            for z in range(zs // 2):
                rows = [((y * zs + half) * xs + x) * share for half in (z, z + zs // 2)]
                start = (y * xs + x) * chunk + (zs + z) * share
                out_ref[start : start + share, :] = jnp.where(
                    low, tail_ref[rows[0] : rows[0] + share, :], tail_ref[rows[1] : rows[1] + share, :]
                ).astype(jnp.bfloat16)


def fold_kernel(share, zs, terms_ref, out_ref):
    total = terms_ref[0].astype(jnp.float32)
    for index in range(1, terms_ref.shape[0]):
        total = total + terms_ref[index].astype(jnp.float32)
    for z in range(zs):
        out_ref[z, :share, :] = total[z * share : (z + 1) * share].astype(jnp.bfloat16)
        first = (zs + z % (zs // 2)) * share
        out_ref[z, share:, :] = total[first : first + share].astype(jnp.bfloat16)


def in_vmem(kernel, shapes, count, limit, scratch=()):
    spec = pl.BlockSpec(memory_space=pltpu.VMEM)
    return pl.pallas_call(
        kernel,
        out_shape=shapes,
        in_specs=[spec] * count,
        out_specs=jax.tree.map(lambda _: spec, shapes),
        scratch_shapes=scratch,
        compiler_params=pltpu.CompilerParams(vmem_limit_bytes=limit),
    )


def per_device(
    activations,
    conv_weight,
    head_first,
    head_second,
    hidden_cotangent,
    score_cotangent,
    donor_row,
    acceptor_owner,
    acceptor_row,
):
    row_count = activations.shape[1]
    chan_count = activations.shape[2]
    out_count = conv_weight.shape[1]
    tap_count = conv_weight.shape[0] // chan_count
    reach_rows = (tap_count - 1) // 2 * DILATION
    shards = lax.axis_size("seq")
    dp_count = lax.axis_size("dp")
    pair_count = donor_row.shape[1]
    capacity = max(2, 2 * pair_count // shards)
    slots = shards * capacity
    col_width = out_count // dp_count

    above, below = seq_halo(activations[0], reach_rows)
    owner = acceptor_owner[0, :, 0]
    pair_ids = jnp.arange(pair_count, dtype=jnp.int32)
    rank = jnp.sum(
        ((owner[:, None] == owner[None, :]) & (pair_ids[None, :] < pair_ids[:, None])).astype(
            jnp.int32
        ),
        axis=1,
    )
    target = owner * capacity + rank
    placed = target[None, :] == jnp.arange(slots, dtype=jnp.int32)[:, None]
    score = score_cotangent[0]
    high = lax.reduce_precision(score, 8, 7)
    middle = lax.reduce_precision(score - high, 8, 7)
    note = jnp.stack([acceptor_row[0].astype(jnp.float32) + 1.0, high, middle, score - high - middle])
    note = jnp.pad(note, ((0, LANES - note.shape[0]), (0, 0))).astype(jnp.bfloat16)
    notes = lax.dot_general(
        placed.astype(jnp.bfloat16), note, (((1,), (1,)), ((), ())), preferred_element_type=jnp.float32
    )
    notes = (notes - (jnp.arange(LANES) == 0).astype(jnp.float32)[None, :]).astype(jnp.bfloat16)
    donor_slot = (
        jnp.sum(jnp.where(placed, donor_row[0][None, :] + 1, 0), axis=1, dtype=jnp.int32) - 1
    )
    row_ids = jnp.arange(row_count, dtype=jnp.int32)
    hits = (donor_slot[:, None] == row_ids[None, :]).astype(jnp.bfloat16)
    hits, notes = lax.optimization_barrier((hits, notes))

    padded_input = jnp.concatenate([above, activations[0], below], axis=0)
    core_input, z_input = swap_core(padded_input), swap_z(padded_input)
    padded_peers = padded_input, core_input, z_input, swap_core(z_input)

    spec, far = pl.BlockSpec(memory_space=pltpu.VMEM), pl.BlockSpec(memory_space=pltpu.HBM)
    padded, hidden, slope, sent = pl.pallas_call(
        functools.partial(conv_kernel, tap_count),
        out_shape=(
            jax.ShapeDtypeStruct((row_count + 2 * reach_rows, chan_count), jnp.bfloat16),
            jax.ShapeDtypeStruct((row_count, out_count), jnp.bfloat16),
            jax.ShapeDtypeStruct((row_count, out_count), jnp.float32),
            jax.ShapeDtypeStruct((slots, out_count + LANES), jnp.bfloat16),
        ),
        in_specs=[spec] * 5 + [far],
        out_specs=(far,) * 3 + (spec,),
        scratch_shapes=[
            pltpu.VMEM(conv_weight.shape, jnp.bfloat16),
            pltpu.VMEM((row_count + 2 * reach_rows, chan_count), jnp.bfloat16),
            pltpu.VMEM((row_count, out_count), jnp.bfloat16),
            pltpu.VMEM((row_count, out_count), jnp.float32),
            pltpu.SemaphoreType.DMA((tap_count + 3,)),
        ],
        compiler_params=pltpu.CompilerParams(vmem_limit_bytes=KERNEL_VMEM),
    )(above, activations[0], below, hits, notes, conv_weight)
    got = lax.all_to_all(
        sent.reshape(shards, capacity, out_count + LANES),
        "seq",
        split_axis=0,
        concat_axis=0,
        tiled=True,
    ).reshape(slots, out_count + LANES)
    slot_shape = jax.ShapeDtypeStruct((slots, out_count), jnp.bfloat16)
    back, part, feature, delta = pl.pallas_call(
        pair_kernel,
        out_shape=(
            slot_shape,
            jax.ShapeDtypeStruct((row_count, out_count), jnp.float32),
            slot_shape,
            slot_shape,
        ),
        in_specs=[spec, far, spec, spec, spec],
        out_specs=(spec, far, spec, spec),
        scratch_shapes=[
            pltpu.VMEM((row_count, out_count), jnp.bfloat16),
            pltpu.VMEM((row_count, out_count), jnp.float32),
            pltpu.SemaphoreType.DMA((2,)),
        ],
        compiler_params=pltpu.CompilerParams(vmem_limit_bytes=KERNEL_VMEM),
    )(got, hidden, head_first, head_second.reshape(1, out_count), hidden_cotangent[0])
    donor_grad = lax.all_to_all(
        back.reshape(shards, capacity, out_count),
        "seq",
        split_axis=0,
        concat_axis=0,
        tiled=True,
    ).reshape(slots, out_count)
    feature_peers = dp_peers(feature)
    delta_peers = dp_columns(delta, col_width)
    head_term = in_vmem(
        functools.partial(head_kernel, 1.0 / math.sqrt(dp_count * pair_count * shards)),
        jax.ShapeDtypeStruct((out_count, col_width), jnp.bfloat16),
        8,
        KERNEL_VMEM,
    )(*feature_peers, *delta_peers)
    hidden_grad = part + contract_rows(hits, donor_grad)
    preact_grad = (hidden_grad * slope).astype(jnp.bfloat16)
    grad_peers = dp_columns(preact_grad, col_width)

    normed_all = in_vmem(
        turn_kernel,
        jax.ShapeDtypeStruct((chan_count, dp_count * (row_count + 2 * reach_rows)), jnp.bfloat16),
        4,
        KERNEL_VMEM,
    )(padded, *padded_peers[1:])
    ys, zs, xs = SEQ_GRID
    row_total = tap_count * chan_count + out_count
    share = row_total // shards
    chunk = share * zs + share * zs // 2
    term = in_vmem(
        functools.partial(
            weight_kernel, 1.0 / math.sqrt(dp_count * row_count * shards), tap_count, SEQ_GRID
        ),
        jax.ShapeDtypeStruct((ys * xs * chunk, LANES), jnp.bfloat16),
        6,
        KERNEL_VMEM,
        [pltpu.VMEM((row_total, LANES), jnp.float32)],
    )(normed_all, head_term, *grad_peers)
    terms = lax.all_to_all(
        term.reshape(ys * xs, chunk, LANES),
        "seq",
        split_axis=0,
        concat_axis=0,
        tiled=True,
        axis_index_groups=[
            [(y * zs + z) * xs + x for y in range(ys) for x in range(xs)] for z in range(zs)
        ],
    )
    own_grad = row_grad(preact_grad, conv_weight, tap_count)
    terms, halo_source, own_grad = lax.optimization_barrier((terms, preact_grad, own_grad))
    folded = in_vmem(
        functools.partial(fold_kernel, share, zs),
        jax.ShapeDtypeStruct((zs, 2 * share, LANES), jnp.bfloat16),
        1,
        KERNEL_VMEM,
    )(terms)
    shares = lax.all_to_all(
        folded,
        "seq",
        split_axis=0,
        concat_axis=0,
        tiled=True,
        axis_index_groups=[
            [(y * zs + z) * xs + x for z in range(zs)] for y in range(ys) for x in range(xs)
        ],
    )
    total = jnp.sum(shares.astype(jnp.float32), axis=0)
    upper = lax.axis_index("seq") // xs % zs >= zs // 2
    others = jnp.where(upper, total[share:, LANES // 2 :], total[share:, : LANES // 2])
    weight_grads = jnp.concatenate([total[:share], others], axis=1)

    grad_above, grad_below = seq_halo(halo_source, reach_rows)
    input_grad = norm_grad(
        activations[0], own_grad + edge_grad(grad_above, grad_below, conv_weight, row_count)
    )
    return (input_grad.astype(jnp.bfloat16)[None], weight_grads)


def against_weights(grads, conv_weight):
    return lax.dot_general(
        grads, conv_weight, (((1,), (1,)), ((), ())), preferred_element_type=jnp.float32
    )


def row_grad(preact_grad, conv_weight, tap_count):
    chan_count = conv_weight.shape[0] // tap_count
    reach = (tap_count - 1) // 2 * DILATION
    row_count = preact_grad.shape[0]
    spread = jnp.pad(against_weights(preact_grad, conv_weight), ((reach, reach), (0, 0)))
    total = None
    for k in range(tap_count):
        first = 2 * reach - k * DILATION
        term = spread[first : first + row_count, k * chan_count : (k + 1) * chan_count]
        total = term if total is None else total + term
    return total


def edge_grad(grad_above, grad_below, conv_weight, row_count):
    width = grad_above.shape[0]
    chan_count = grad_above.shape[1]
    spread = against_weights(jnp.concatenate([grad_above, grad_below], axis=0), conv_weight)

    def tap(k):
        return spread[:, k * chan_count : (k + 1) * chan_count]

    none = jnp.zeros((width - DILATION, chan_count), jnp.float32)
    top = tap(4)[:width] + jnp.concatenate([tap(3)[DILATION:width], none], axis=0)
    bottom = tap(0)[width:] + jnp.concatenate([none, tap(1)[width : 2 * width - DILATION]], axis=0)
    middle = jnp.zeros((row_count - 2 * width, chan_count), jnp.float32)
    return jnp.concatenate([top, middle, bottom], axis=0)


def norm_grad(inputs, normed_grad):
    values = inputs.astype(jnp.float32)
    inverse = lax.rsqrt(jnp.mean(values * values, axis=1, keepdims=True) + 1e-05)
    return inverse * normed_grad - values * inverse**3 * jnp.mean(
        normed_grad * values, axis=1, keepdims=True
    )


def solution(mesh):
    placed = (
        P("dp", "seq", None),
        P(),
        P(),
        P(),
        P("dp", "seq", None),
        P("dp", "seq"),
        P("dp", "seq"),
        P("dp", "seq", None),
        P("dp", "seq"),
    )

    return jax.shard_map(
        per_device,
        mesh=mesh,
        in_specs=placed,
        out_specs=(P("dp", "seq", None), P("seq", "dp")),
        check_vma=False,
    )
```

```python
import functools
import math

import jax
import jax.numpy as jnp
from jax import lax
from jax.experimental import pallas as pl
from jax.experimental.pallas import tpu as pltpu
from jax.sharding import PartitionSpec as P


DILATION = 8
LANES = 128
SEQ_GRID = (4, 4, 4)
KERNEL_VMEM = 16 * 1024 * 1024


def gelu_slope(values):
    normal_cdf = 0.5 * (1.0 + lax.erf(values * (1.0 / math.sqrt(2.0))))
    density = jnp.exp(-0.5 * values * values) * (1.0 / math.sqrt(2.0 * math.pi))
    return normal_cdf + values * density


def contract_rows(left_side, right_side):
    return lax.dot_general(
        left_side, right_side, (((0,), (0,)), ((), ())), preferred_element_type=jnp.float32
    )


def seq_halo(cells, width):
    count = lax.axis_size("seq")
    above = lax.ppermute(cells[-width:], "seq", [(i, i + 1) for i in range(count - 1)])
    below = lax.ppermute(cells[:width], "seq", [(i + 1, i) for i in range(count - 1)])
    return above, below


def swap_core(field):
    return lax.ppermute(field, "dp", [(0, 1), (1, 0), (2, 3), (3, 2)])


def swap_z(field):
    return lax.ppermute(field, "dp", [(0, 2), (1, 3), (2, 0), (3, 1)])


def dp_columns(field, width):
    index = lax.axis_index("dp")
    found = []
    for flip in range(4):
        piece = lax.dynamic_slice_in_dim(field, (index ^ flip) * width, width, axis=1)
        if flip:
            piece = lax.ppermute(piece, "dp", [(i, i ^ flip) for i in range(4)])
        found.append(piece)
    return found


def tail_twice(values):
    return jnp.concatenate([values, values[:, LANES:]], axis=1)


def conv_kernel(taps, above_ref, input_ref, below_ref, hits_ref, notes_ref, weight_ref, *rest):
    padded_out, hidden_out, slope_out, sent_ref, held_ref, padded_ref, hidden_ref, slope_ref, done = rest
    row_count, chan_count = input_ref.shape
    leaving = [
        pltpu.make_async_copy(source, target, done.at[taps + index])
        for index, (source, target) in enumerate(
            ((padded_ref, padded_out), (hidden_ref, hidden_out), (slope_ref, slope_out))
        )
    ]
    copies = []
    for k in range(taps):
        rows = pl.ds(k * chan_count, chan_count)
        copies.append(pltpu.make_async_copy(weight_ref.at[rows], held_ref.at[rows], done.at[k]))
        copies[-1].start()
    values = jnp.concatenate([above_ref[...], input_ref[...], below_ref[...]], axis=0).astype(
        jnp.float32
    )
    inverse = lax.rsqrt(jnp.mean(values * values, axis=1, keepdims=True) + 1e-05)
    normed = values * inverse
    padded_ref[...] = normed.astype(jnp.bfloat16)
    leaving[0].start()
    preact = jnp.zeros((row_count, hidden_ref.shape[1]), jnp.float32)
    for k in range(taps):
        column = normed[k * DILATION : k * DILATION + row_count].astype(jnp.bfloat16)
        copies[k].wait()
        preact = preact + jnp.dot(
            column,
            held_ref[k * chan_count : (k + 1) * chan_count, :],
            preferred_element_type=jnp.float32,
        )
    normal_cdf = 0.5 * (1.0 + lax.erf(preact * (1.0 / math.sqrt(2.0))))
    density = jnp.exp(-0.5 * preact * preact) * (1.0 / math.sqrt(2.0 * math.pi))
    hidden = (preact * normal_cdf).astype(jnp.bfloat16)
    hidden_ref[...] = hidden
    leaving[1].start()
    slope_ref[...] = normal_cdf + preact * density
    leaving[2].start()
    out_count = hidden_ref.shape[1]
    sent_ref[:, :out_count] = jnp.dot(
        hits_ref[...], hidden, preferred_element_type=jnp.float32
    ).astype(jnp.bfloat16)
    sent_ref[:, out_count:] = notes_ref[...]
    for copy in leaving:
        copy.wait()


def turn_kernel(own_ref, *refs):
    peers, out_ref = refs[:-1], refs[-1]
    pieces = [own_ref[...].astype(jnp.float32)]
    for peer in peers:
        values = peer[...].astype(jnp.float32)
        inverse = lax.rsqrt(jnp.mean(values * values, axis=1, keepdims=True) + 1e-05)
        pieces.append(values * inverse)
    out_ref[...] = jnp.concatenate(pieces, axis=0).T.astype(jnp.bfloat16)


def pair_kernel(got_ref, hidden_in, first_ref, second_ref, cotangent_ref, *rest):
    back_ref, part_out, feature_ref, delta_ref, hidden_ref, part_ref, done = rest
    hidden_copy = pltpu.make_async_copy(hidden_in, hidden_ref, done.at[0])
    part_copy = pltpu.make_async_copy(part_ref, part_out, done.at[1])
    hidden_copy.start()
    chan_count = hidden_ref.shape[1]
    slots = got_ref.shape[0]
    note = got_ref[:, chan_count:].astype(jnp.float32)
    score = note[:, 1:2] + note[:, 2:3] + note[:, 3:4]
    row_ids = lax.broadcasted_iota(jnp.int32, (slots, hidden_ref.shape[0]), 1).astype(jnp.float32)
    hits = (note[:, 0:1] == row_ids).astype(jnp.float32).astype(jnp.bfloat16)
    hidden_copy.wait()
    accept = jnp.dot(hits, hidden_ref[...], preferred_element_type=jnp.float32)
    donor = got_ref[:, :chan_count].astype(jnp.float32)
    feature = (donor * accept).astype(jnp.bfloat16)
    feature_ref[...] = feature
    head_preact = jnp.dot(feature, first_ref[...], preferred_element_type=jnp.float32)
    delta = (score * second_ref[...].astype(jnp.float32) * gelu_slope(head_preact)).astype(
        jnp.bfloat16
    )
    delta_ref[...] = delta
    feature_grad = lax.dot_general(
        delta, first_ref[...], (((1,), (1,)), ((), ())), preferred_element_type=jnp.float32
    )
    accept_grad = (feature_grad * donor).astype(jnp.bfloat16)
    part_ref[...] = cotangent_ref[...].astype(jnp.float32) + contract_rows(hits, accept_grad)
    part_copy.start()
    back_ref[...] = (feature_grad * accept).astype(jnp.bfloat16)
    part_copy.wait()


def head_kernel(scale, feature_ref, feature_core_ref, *refs):
    for own, core, out in zip(refs[0:2], refs[2:4], refs[4:6], strict=True):
        term = contract_rows(own[...], feature_ref[...]) + contract_rows(
            core[...], feature_core_ref[...]
        )
        out[...] = (term.T * scale).astype(jnp.bfloat16)


def weight_kernel(scale, taps, grid, *refs):
    normed_ref, heads, grads, out_ref, tail_ref = refs[0], refs[1:3], refs[3:7], refs[7], refs[8]
    ys, zs, xs = grid
    chan_count = normed_ref.shape[0]
    width = 2 * LANES
    reach = (taps - 1) * DILATION
    share = tail_ref.shape[0] // (ys * zs * xs)
    chunk = share * zs + share * zs // 2
    values = [tail_twice(ref[...].astype(jnp.float32)) for ref in grads]

    def put(first, block):
        tail_ref[first : first + block.shape[0], :] = block[:, LANES:]
        done = 0
        while done < block.shape[0]:
            owner, inside = divmod(first + done, share)
            step = min(share - inside, block.shape[0] - done)
            y, z, x = owner // (zs * xs), owner // xs % zs, owner % xs
            start = (y * xs + x) * chunk + z * share + inside
            out_ref[start : start + step, :] = block[done : done + step, :LANES].astype(jnp.bfloat16)
            done += step

    for k in range(taps):
        pieces = []
        for value in values:
            if k:
                pieces.append(jnp.zeros((k * DILATION, width), jnp.float32))
            pieces.append(value)
            if k < taps - 1:
                pieces.append(jnp.zeros((reach - k * DILATION, width), jnp.float32))
        shifted = jnp.concatenate(pieces, axis=0).astype(jnp.bfloat16)
        put(
            k * chan_count,
            jnp.dot(normed_ref[...], shifted, preferred_element_type=jnp.float32) * scale,
        )
    head_term = heads[0][...].astype(jnp.float32) + heads[1][...].astype(jnp.float32)
    put(taps * chan_count, tail_twice(head_term))
    low = lax.broadcasted_iota(jnp.int32, (share, LANES), 1) < LANES // 2
    for y in range(ys):
        for x in range(xs):
            for z in range(zs // 2):
                rows = [((y * zs + half) * xs + x) * share for half in (z, z + zs // 2)]
                start = (y * xs + x) * chunk + (zs + z) * share
                out_ref[start : start + share, :] = jnp.where(
                    low, tail_ref[rows[0] : rows[0] + share, :], tail_ref[rows[1] : rows[1] + share, :]
                ).astype(jnp.bfloat16)


def fold_kernel(share, zs, terms_ref, out_ref):
    total = terms_ref[0].astype(jnp.float32)
    for index in range(1, terms_ref.shape[0]):
        total = total + terms_ref[index].astype(jnp.float32)
    for z in range(zs):
        out_ref[z, :share, :] = total[z * share : (z + 1) * share].astype(jnp.bfloat16)
        first = (zs + z % (zs // 2)) * share
        out_ref[z, share:, :] = total[first : first + share].astype(jnp.bfloat16)


def in_vmem(kernel, shapes, count, limit, scratch=()):
    spec = pl.BlockSpec(memory_space=pltpu.VMEM)
    return pl.pallas_call(
        kernel,
        out_shape=shapes,
        in_specs=[spec] * count,
        out_specs=jax.tree.map(lambda _: spec, shapes),
        scratch_shapes=scratch,
        compiler_params=pltpu.CompilerParams(vmem_limit_bytes=limit),
    )


def per_device(
    activations,
    conv_weight,
    head_first,
    head_second,
    hidden_cotangent,
    score_cotangent,
    donor_row,
    acceptor_owner,
    acceptor_row,
):
    row_count = activations.shape[1]
    chan_count = activations.shape[2]
    out_count = conv_weight.shape[1]
    tap_count = conv_weight.shape[0] // chan_count
    reach_rows = (tap_count - 1) // 2 * DILATION
    shards = lax.axis_size("seq")
    dp_count = lax.axis_size("dp")
    pair_count = donor_row.shape[1]
    capacity = max(2, 2 * pair_count // shards)
    slots = shards * capacity
    col_width = out_count // dp_count

    above, below = seq_halo(activations[0], reach_rows)
    owner = acceptor_owner[0, :, 0]
    pair_ids = jnp.arange(pair_count, dtype=jnp.int32)
    rank = jnp.sum(
        ((owner[:, None] == owner[None, :]) & (pair_ids[None, :] < pair_ids[:, None])).astype(
            jnp.int32
        ),
        axis=1,
    )
    target = owner * capacity + rank
    placed = target[None, :] == jnp.arange(slots, dtype=jnp.int32)[:, None]
    score = score_cotangent[0]
    high = lax.reduce_precision(score, 8, 7)
    middle = lax.reduce_precision(score - high, 8, 7)
    note = jnp.stack([acceptor_row[0].astype(jnp.float32) + 1.0, high, middle, score - high - middle])
    note = jnp.pad(note, ((0, LANES - note.shape[0]), (0, 0))).astype(jnp.bfloat16)
    notes = lax.dot_general(
        placed.astype(jnp.bfloat16), note, (((1,), (1,)), ((), ())), preferred_element_type=jnp.float32
    )
    notes = (notes - (jnp.arange(LANES) == 0).astype(jnp.float32)[None, :]).astype(jnp.bfloat16)
    donor_slot = (
        jnp.sum(jnp.where(placed, donor_row[0][None, :] + 1, 0), axis=1, dtype=jnp.int32) - 1
    )
    row_ids = jnp.arange(row_count, dtype=jnp.int32)
    hits = (donor_slot[:, None] == row_ids[None, :]).astype(jnp.bfloat16)
    hits, notes = lax.optimization_barrier((hits, notes))

    padded_input = jnp.concatenate([above, activations[0], below], axis=0)
    core_input, z_input = swap_core(padded_input), swap_z(padded_input)
    padded_peers = padded_input, core_input, z_input, swap_core(z_input)

    spec, far = pl.BlockSpec(memory_space=pltpu.VMEM), pl.BlockSpec(memory_space=pltpu.HBM)
    padded, hidden, slope, sent = pl.pallas_call(
        functools.partial(conv_kernel, tap_count),
        out_shape=(
            jax.ShapeDtypeStruct((row_count + 2 * reach_rows, chan_count), jnp.bfloat16),
            jax.ShapeDtypeStruct((row_count, out_count), jnp.bfloat16),
            jax.ShapeDtypeStruct((row_count, out_count), jnp.float32),
            jax.ShapeDtypeStruct((slots, out_count + LANES), jnp.bfloat16),
        ),
        in_specs=[spec] * 5 + [far],
        out_specs=(far,) * 3 + (spec,),
        scratch_shapes=[
            pltpu.VMEM(conv_weight.shape, jnp.bfloat16),
            pltpu.VMEM((row_count + 2 * reach_rows, chan_count), jnp.bfloat16),
            pltpu.VMEM((row_count, out_count), jnp.bfloat16),
            pltpu.VMEM((row_count, out_count), jnp.float32),
            pltpu.SemaphoreType.DMA((tap_count + 3,)),
        ],
        compiler_params=pltpu.CompilerParams(vmem_limit_bytes=KERNEL_VMEM),
    )(above, activations[0], below, hits, notes, conv_weight)
    got = lax.all_to_all(
        sent.reshape(shards, capacity, out_count + LANES),
        "seq",
        split_axis=0,
        concat_axis=0,
        tiled=True,
    ).reshape(slots, out_count + LANES)
    slot_shape = jax.ShapeDtypeStruct((slots, out_count), jnp.bfloat16)
    back, part, feature, delta = pl.pallas_call(
        pair_kernel,
        out_shape=(
            slot_shape,
            jax.ShapeDtypeStruct((row_count, out_count), jnp.float32),
            slot_shape,
            slot_shape,
        ),
        in_specs=[spec, far, spec, spec, spec],
        out_specs=(spec, far, spec, spec),
        scratch_shapes=[
            pltpu.VMEM((row_count, out_count), jnp.bfloat16),
            pltpu.VMEM((row_count, out_count), jnp.float32),
            pltpu.SemaphoreType.DMA((2,)),
        ],
        compiler_params=pltpu.CompilerParams(vmem_limit_bytes=KERNEL_VMEM),
    )(got, hidden, head_first, head_second.reshape(1, out_count), hidden_cotangent[0])
    donor_grad = lax.all_to_all(
        back.reshape(shards, capacity, out_count),
        "seq",
        split_axis=0,
        concat_axis=0,
        tiled=True,
    ).reshape(slots, out_count)
    own_place = lax.axis_index("dp")
    delta_cols = [
        lax.dynamic_slice_in_dim(delta, (own_place ^ flip) * col_width, col_width, axis=1)
        for flip in (0, 2, 1, 3)
    ]
    feature_core = swap_core(feature)
    delta_core = [swap_core(piece) for piece in delta_cols[2:]]
    head_shape = jax.ShapeDtypeStruct((out_count, col_width), jnp.bfloat16)
    head_kept, head_away = in_vmem(
        functools.partial(head_kernel, 1.0 / math.sqrt(dp_count * pair_count * shards)),
        (head_shape, head_shape),
        6,
        KERNEL_VMEM,
    )(feature, feature_core, *delta_cols[:2], *delta_core)
    head_got = swap_z(head_away)
    hidden_grad = part + contract_rows(hits, donor_grad)
    preact_grad = (hidden_grad * slope).astype(jnp.bfloat16)
    grad_peers = dp_columns(preact_grad, col_width)
    grad_above, grad_below = seq_halo(preact_grad, reach_rows)

    normed_all = in_vmem(
        turn_kernel,
        jax.ShapeDtypeStruct((chan_count, dp_count * (row_count + 2 * reach_rows)), jnp.bfloat16),
        4,
        KERNEL_VMEM,
    )(padded, *padded_peers[1:])
    ys, zs, xs = SEQ_GRID
    row_total = tap_count * chan_count + out_count
    share = row_total // shards
    chunk = share * zs + share * zs // 2
    term = in_vmem(
        functools.partial(
            weight_kernel, 1.0 / math.sqrt(dp_count * row_count * shards), tap_count, SEQ_GRID
        ),
        jax.ShapeDtypeStruct((ys * xs * chunk, LANES), jnp.bfloat16),
        7,
        KERNEL_VMEM,
        [pltpu.VMEM((row_total, LANES), jnp.float32)],
    )(normed_all, head_kept, head_got, *grad_peers)
    terms = lax.all_to_all(
        term.reshape(ys * xs, chunk, LANES),
        "seq",
        split_axis=0,
        concat_axis=0,
        tiled=True,
        axis_index_groups=[
            [(y * zs + z) * xs + x for y in range(ys) for x in range(xs)] for z in range(zs)
        ],
    )
    folded = in_vmem(
        functools.partial(fold_kernel, share, zs),
        jax.ShapeDtypeStruct((zs, 2 * share, LANES), jnp.bfloat16),
        1,
        KERNEL_VMEM,
    )(terms)
    shares = lax.all_to_all(
        folded,
        "seq",
        split_axis=0,
        concat_axis=0,
        tiled=True,
        axis_index_groups=[
            [(y * zs + z) * xs + x for z in range(zs)] for y in range(ys) for x in range(xs)
        ],
    )
    total = jnp.sum(shares.astype(jnp.float32), axis=0)
    upper = lax.axis_index("seq") // xs % zs >= zs // 2
    others = jnp.where(upper, total[share:, LANES // 2 :], total[share:, : LANES // 2])
    weight_grads = jnp.concatenate([total[:share], others], axis=1)

    input_grad = data_grad(
        activations[0], grad_above, preact_grad, grad_below, conv_weight, tap_count
    )
    return (input_grad.astype(jnp.bfloat16)[None], weight_grads)


def data_grad(inputs, grad_above, preact_grad, grad_below, conv_weight, tap_count):
    reach_rows = grad_above.shape[0]
    row_count, chan_count = inputs.shape
    input_values = inputs.astype(jnp.float32)
    norm_inverse = lax.rsqrt(
        jnp.mean(input_values * input_values, axis=1, keepdims=True) + 1e-05
    )
    grad_padded = jnp.concatenate([grad_above, preact_grad, grad_below], axis=0)
    spread = lax.dot_general(
        grad_padded, conv_weight, (((1,), (1,)), ((), ())), preferred_element_type=jnp.float32
    )
    normed_grad = spread[2 * reach_rows : 2 * reach_rows + row_count, 0:chan_count]
    for tap_index in range(1, tap_count):
        first_row = 2 * reach_rows - tap_index * DILATION
        normed_grad = (
            normed_grad
            + spread[
                first_row : first_row + row_count,
                tap_index * chan_count : (tap_index + 1) * chan_count,
            ]
        )
    return norm_inverse * normed_grad - input_values * norm_inverse**3 * jnp.mean(
        normed_grad * input_values, axis=1, keepdims=True
    )


def solution(mesh):
    placed = (
        P("dp", "seq", None),
        P(),
        P(),
        P(),
        P("dp", "seq", None),
        P("dp", "seq"),
        P("dp", "seq"),
        P("dp", "seq", None),
        P("dp", "seq"),
    )

    return jax.shard_map(
        per_device,
        mesh=mesh,
        in_specs=placed,
        out_specs=(P("dp", "seq", None), P("seq", "dp")),
        check_vma=False,
    )
```

```python
import functools
import math

import jax
import jax.numpy as jnp
from jax import lax
from jax.experimental import pallas as pl
from jax.experimental.pallas import tpu as pltpu
from jax.sharding import PartitionSpec as P


DILATION = 8
LANES = 128
SEQ_GRID = (4, 4, 4)
KERNEL_VMEM = 16 * 1024 * 1024


def gelu_slope(values):
    normal_cdf = 0.5 * (1.0 + lax.erf(values * (1.0 / math.sqrt(2.0))))
    density = jnp.exp(-0.5 * values * values) * (1.0 / math.sqrt(2.0 * math.pi))
    return normal_cdf + values * density


def contract_rows(left_side, right_side):
    return lax.dot_general(
        left_side, right_side, (((0,), (0,)), ((), ())), preferred_element_type=jnp.float32
    )


def seq_halo(cells, width):
    count = lax.axis_size("seq")
    above = lax.ppermute(cells[-width:], "seq", [(i, i + 1) for i in range(count - 1)])
    below = lax.ppermute(cells[:width], "seq", [(i + 1, i) for i in range(count - 1)])
    return above, below


def swap_core(field):
    return lax.ppermute(field, "dp", [(0, 1), (1, 0), (2, 3), (3, 2)])


def swap_z(field):
    return lax.ppermute(field, "dp", [(0, 2), (1, 3), (2, 0), (3, 1)])


def dp_columns(field, width):
    index = lax.axis_index("dp")
    found = []
    for flip in range(4):
        piece = lax.dynamic_slice_in_dim(field, (index ^ flip) * width, width, axis=1)
        if flip:
            piece = lax.ppermute(piece, "dp", [(i, i ^ flip) for i in range(4)])
        found.append(piece)
    return found


def tail_twice(values):
    return jnp.concatenate([values, values[:, LANES:]], axis=1)


def conv_kernel(taps, above_ref, below_ref, hits_ref, notes_ref, input_in, weight_ref, *rest):
    padded_out, hidden_out, slope_out, sent_ref = rest[:4]
    held_ref, input_ref, padded_ref, hidden_ref, slope_ref, done = rest[4:]
    row_count, chan_count = input_ref.shape
    input_copy = pltpu.make_async_copy(input_in, input_ref, done.at[taps + 3])
    input_copy.start()
    leaving = [
        pltpu.make_async_copy(source, target, done.at[taps + index])
        for index, (source, target) in enumerate(
            ((padded_ref, padded_out), (hidden_ref, hidden_out), (slope_ref, slope_out))
        )
    ]
    copies = []
    for k in range(taps):
        rows = pl.ds(k * chan_count, chan_count)
        copies.append(pltpu.make_async_copy(weight_ref.at[rows], held_ref.at[rows], done.at[k]))
        copies[-1].start()
    input_copy.wait()
    values = jnp.concatenate([above_ref[...], input_ref[...], below_ref[...]], axis=0).astype(
        jnp.float32
    )
    inverse = lax.rsqrt(jnp.mean(values * values, axis=1, keepdims=True) + 1e-05)
    normed = values * inverse
    padded_ref[...] = normed.astype(jnp.bfloat16)
    leaving[0].start()
    preact = jnp.zeros((row_count, hidden_ref.shape[1]), jnp.float32)
    for k in range(taps):
        column = normed[k * DILATION : k * DILATION + row_count].astype(jnp.bfloat16)
        copies[k].wait()
        preact = preact + jnp.dot(
            column,
            held_ref[k * chan_count : (k + 1) * chan_count, :],
            preferred_element_type=jnp.float32,
        )
    normal_cdf = 0.5 * (1.0 + lax.erf(preact * (1.0 / math.sqrt(2.0))))
    density = jnp.exp(-0.5 * preact * preact) * (1.0 / math.sqrt(2.0 * math.pi))
    hidden = (preact * normal_cdf).astype(jnp.bfloat16)
    hidden_ref[...] = hidden
    leaving[1].start()
    slope_ref[...] = normal_cdf + preact * density
    leaving[2].start()
    out_count = hidden_ref.shape[1]
    sent_ref[:, :out_count] = jnp.dot(
        hits_ref[...], hidden, preferred_element_type=jnp.float32
    ).astype(jnp.bfloat16)
    sent_ref[:, out_count:] = notes_ref[...]
    for copy in leaving:
        copy.wait()


def turn_kernel(own_ref, *refs):
    peers, out_ref = refs[:-1], refs[-1]
    pieces = [own_ref[...].astype(jnp.float32)]
    for peer in peers:
        values = peer[...].astype(jnp.float32)
        inverse = lax.rsqrt(jnp.mean(values * values, axis=1, keepdims=True) + 1e-05)
        pieces.append(values * inverse)
    out_ref[...] = jnp.concatenate(pieces, axis=0).T.astype(jnp.bfloat16)


def pair_kernel(got_ref, hidden_in, first_ref, second_ref, cotangent_in, *rest):
    back_ref, part_out, feature_ref, delta_ref = rest[:4]
    hidden_ref, cotangent_ref, part_ref, done = rest[4:]
    cotangent_copy = pltpu.make_async_copy(cotangent_in, cotangent_ref, done.at[2])
    hidden_copy = pltpu.make_async_copy(hidden_in, hidden_ref, done.at[0])
    part_copy = pltpu.make_async_copy(part_ref, part_out, done.at[1])
    hidden_copy.start()
    cotangent_copy.start()
    chan_count = hidden_ref.shape[1]
    slots = got_ref.shape[0]
    note = got_ref[:, chan_count:].astype(jnp.float32)
    score = note[:, 1:2] + note[:, 2:3] + note[:, 3:4]
    row_ids = lax.broadcasted_iota(jnp.int32, (slots, hidden_ref.shape[0]), 1).astype(jnp.float32)
    hits = (note[:, 0:1] == row_ids).astype(jnp.float32).astype(jnp.bfloat16)
    hidden_copy.wait()
    accept = jnp.dot(hits, hidden_ref[...], preferred_element_type=jnp.float32)
    donor = got_ref[:, :chan_count].astype(jnp.float32)
    feature = (donor * accept).astype(jnp.bfloat16)
    feature_ref[...] = feature
    head_preact = jnp.dot(feature, first_ref[...], preferred_element_type=jnp.float32)
    delta = (score * second_ref[...].astype(jnp.float32) * gelu_slope(head_preact)).astype(
        jnp.bfloat16
    )
    delta_ref[...] = delta
    feature_grad = lax.dot_general(
        delta, first_ref[...], (((1,), (1,)), ((), ())), preferred_element_type=jnp.float32
    )
    accept_grad = (feature_grad * donor).astype(jnp.bfloat16)
    cotangent_copy.wait()
    part_ref[...] = cotangent_ref[...].astype(jnp.float32) + contract_rows(hits, accept_grad)
    part_copy.start()
    back_ref[...] = (feature_grad * accept).astype(jnp.bfloat16)
    part_copy.wait()


def head_kernel(scale, feature_ref, feature_core_ref, *refs):
    for own, core, out in zip(refs[0:2], refs[2:4], refs[4:6], strict=True):
        term = contract_rows(own[...], feature_ref[...]) + contract_rows(
            core[...], feature_core_ref[...]
        )
        out[...] = (term.T * scale).astype(jnp.bfloat16)


def weight_kernel(scale, taps, grid, *refs):
    normed_ref, heads, grads, out_ref, tail_ref = refs[0], refs[1:3], refs[3:7], refs[7], refs[8]
    ys, zs, xs = grid
    chan_count = normed_ref.shape[0]
    width = 2 * LANES
    reach = (taps - 1) * DILATION
    share = tail_ref.shape[0] // (ys * zs * xs)
    chunk = share * zs + share * zs // 2
    values = [tail_twice(ref[...].astype(jnp.float32)) for ref in grads]

    def put(first, block):
        tail_ref[first : first + block.shape[0], :] = block[:, LANES:]
        done = 0
        while done < block.shape[0]:
            owner, inside = divmod(first + done, share)
            step = min(share - inside, block.shape[0] - done)
            y, z, x = owner // (zs * xs), owner // xs % zs, owner % xs
            start = (y * xs + x) * chunk + z * share + inside
            out_ref[start : start + step, :] = block[done : done + step, :LANES].astype(jnp.bfloat16)
            done += step

    for k in range(taps):
        pieces = []
        for value in values:
            if k:
                pieces.append(jnp.zeros((k * DILATION, width), jnp.float32))
            pieces.append(value)
            if k < taps - 1:
                pieces.append(jnp.zeros((reach - k * DILATION, width), jnp.float32))
        shifted = jnp.concatenate(pieces, axis=0).astype(jnp.bfloat16)
        put(
            k * chan_count,
            jnp.dot(normed_ref[...], shifted, preferred_element_type=jnp.float32) * scale,
        )
    head_term = heads[0][...].astype(jnp.float32) + heads[1][...].astype(jnp.float32)
    put(taps * chan_count, tail_twice(head_term))
    low = lax.broadcasted_iota(jnp.int32, (share, LANES), 1) < LANES // 2
    for y in range(ys):
        for x in range(xs):
            for z in range(zs // 2):
                rows = [((y * zs + half) * xs + x) * share for half in (z, z + zs // 2)]
                start = (y * xs + x) * chunk + (zs + z) * share
                out_ref[start : start + share, :] = jnp.where(
                    low, tail_ref[rows[0] : rows[0] + share, :], tail_ref[rows[1] : rows[1] + share, :]
                ).astype(jnp.bfloat16)


def fold_kernel(share, zs, terms_ref, out_ref):
    total = terms_ref[0].astype(jnp.float32)
    for index in range(1, terms_ref.shape[0]):
        total = total + terms_ref[index].astype(jnp.float32)
    for z in range(zs):
        out_ref[z, :share, :] = total[z * share : (z + 1) * share].astype(jnp.bfloat16)
        first = (zs + z % (zs // 2)) * share
        out_ref[z, share:, :] = total[first : first + share].astype(jnp.bfloat16)


def in_hbm(field):
    return pltpu.with_memory_space_constraint(field, pltpu.HBM)


def in_vmem(kernel, shapes, count, limit, scratch=()):
    spec = pl.BlockSpec(memory_space=pltpu.VMEM)
    return pl.pallas_call(
        kernel,
        out_shape=shapes,
        in_specs=[spec] * count,
        out_specs=jax.tree.map(lambda _: spec, shapes),
        scratch_shapes=scratch,
        compiler_params=pltpu.CompilerParams(vmem_limit_bytes=limit),
    )


def per_device(
    activations,
    conv_weight,
    head_first,
    head_second,
    hidden_cotangent,
    score_cotangent,
    donor_row,
    acceptor_owner,
    acceptor_row,
):
    row_count = activations.shape[1]
    chan_count = activations.shape[2]
    out_count = conv_weight.shape[1]
    tap_count = conv_weight.shape[0] // chan_count
    reach_rows = (tap_count - 1) // 2 * DILATION
    shards = lax.axis_size("seq")
    dp_count = lax.axis_size("dp")
    pair_count = donor_row.shape[1]
    capacity = max(2, 2 * pair_count // shards)
    slots = shards * capacity
    col_width = out_count // dp_count

    above, below = seq_halo(activations[0], reach_rows)
    owner = acceptor_owner[0, :, 0]
    pair_ids = jnp.arange(pair_count, dtype=jnp.int32)
    rank = jnp.sum(
        ((owner[:, None] == owner[None, :]) & (pair_ids[None, :] < pair_ids[:, None])).astype(
            jnp.int32
        ),
        axis=1,
    )
    target = owner * capacity + rank
    placed = target[None, :] == jnp.arange(slots, dtype=jnp.int32)[:, None]
    score = score_cotangent[0]
    high = lax.reduce_precision(score, 8, 7)
    middle = lax.reduce_precision(score - high, 8, 7)
    note = jnp.stack([acceptor_row[0].astype(jnp.float32) + 1.0, high, middle, score - high - middle])
    note = jnp.pad(note, ((0, LANES - note.shape[0]), (0, 0))).astype(jnp.bfloat16)
    notes = lax.dot_general(
        placed.astype(jnp.bfloat16), note, (((1,), (1,)), ((), ())), preferred_element_type=jnp.float32
    )
    notes = (notes - (jnp.arange(LANES) == 0).astype(jnp.float32)[None, :]).astype(jnp.bfloat16)
    donor_slot = (
        jnp.sum(jnp.where(placed, donor_row[0][None, :] + 1, 0), axis=1, dtype=jnp.int32) - 1
    )
    row_ids = jnp.arange(row_count, dtype=jnp.int32)
    hits = (donor_slot[:, None] == row_ids[None, :]).astype(jnp.bfloat16)
    hits, notes = lax.optimization_barrier((hits, notes))

    padded_input = jnp.concatenate([above, activations[0], below], axis=0)
    core_input, z_input = swap_core(padded_input), swap_z(padded_input)
    padded_peers = padded_input, core_input, z_input, swap_core(z_input)

    spec, far = pl.BlockSpec(memory_space=pltpu.VMEM), pl.BlockSpec(memory_space=pltpu.HBM)
    padded, hidden, slope, sent = pl.pallas_call(
        functools.partial(conv_kernel, tap_count),
        out_shape=(
            pltpu.HBM((row_count + 2 * reach_rows, chan_count), jnp.bfloat16),
            pltpu.HBM((row_count, out_count), jnp.bfloat16),
            pltpu.HBM((row_count, out_count), jnp.float32),
            jax.ShapeDtypeStruct((slots, out_count + LANES), jnp.bfloat16),
        ),
        in_specs=[spec] * 4 + [far] * 2,
        out_specs=(far,) * 3 + (spec,),
        scratch_shapes=[
            pltpu.VMEM(conv_weight.shape, jnp.bfloat16),
            pltpu.VMEM((row_count, chan_count), jnp.bfloat16),
            pltpu.VMEM((row_count + 2 * reach_rows, chan_count), jnp.bfloat16),
            pltpu.VMEM((row_count, out_count), jnp.bfloat16),
            pltpu.VMEM((row_count, out_count), jnp.float32),
            pltpu.SemaphoreType.DMA((tap_count + 4,)),
        ],
        compiler_params=pltpu.CompilerParams(vmem_limit_bytes=KERNEL_VMEM),
    )(above, below, hits, notes, in_hbm(activations[0]), in_hbm(conv_weight))
    got = lax.all_to_all(
        sent.reshape(shards, capacity, out_count + LANES),
        "seq",
        split_axis=0,
        concat_axis=0,
        tiled=True,
    ).reshape(slots, out_count + LANES)
    slot_shape = jax.ShapeDtypeStruct((slots, out_count), jnp.bfloat16)
    back, part, feature, delta = pl.pallas_call(
        pair_kernel,
        out_shape=(
            slot_shape,
            jax.ShapeDtypeStruct((row_count, out_count), jnp.float32),
            slot_shape,
            slot_shape,
        ),
        in_specs=[spec, far, spec, spec, far],
        out_specs=(spec, far, spec, spec),
        scratch_shapes=[
            pltpu.VMEM((row_count, out_count), jnp.bfloat16),
            pltpu.VMEM((row_count, out_count), jnp.bfloat16),
            pltpu.VMEM((row_count, out_count), jnp.float32),
            pltpu.SemaphoreType.DMA((3,)),
        ],
        compiler_params=pltpu.CompilerParams(vmem_limit_bytes=KERNEL_VMEM),
    )(
        got,
        in_hbm(hidden),
        head_first,
        head_second.reshape(1, out_count),
        in_hbm(hidden_cotangent[0]),
    )
    donor_grad = lax.all_to_all(
        back.reshape(shards, capacity, out_count),
        "seq",
        split_axis=0,
        concat_axis=0,
        tiled=True,
    ).reshape(slots, out_count)
    own_place = lax.axis_index("dp")
    delta_cols = [
        lax.dynamic_slice_in_dim(delta, (own_place ^ flip) * col_width, col_width, axis=1)
        for flip in (0, 2, 1, 3)
    ]
    feature_core = swap_core(feature)
    delta_core = [swap_core(piece) for piece in delta_cols[2:]]
    head_shape = jax.ShapeDtypeStruct((out_count, col_width), jnp.bfloat16)
    head_kept, head_away = in_vmem(
        functools.partial(head_kernel, 1.0 / math.sqrt(dp_count * pair_count * shards)),
        (head_shape, head_shape),
        6,
        KERNEL_VMEM,
    )(feature, feature_core, *delta_cols[:2], *delta_core)
    head_got = swap_z(head_away)
    hidden_grad = part + contract_rows(hits, donor_grad)
    preact_grad = (hidden_grad * slope).astype(jnp.bfloat16)
    grad_peers = dp_columns(preact_grad, col_width)
    grad_above, grad_below = seq_halo(preact_grad, reach_rows)

    normed_all = in_vmem(
        turn_kernel,
        jax.ShapeDtypeStruct((chan_count, dp_count * (row_count + 2 * reach_rows)), jnp.bfloat16),
        4,
        KERNEL_VMEM,
    )(padded, *padded_peers[1:])
    ys, zs, xs = SEQ_GRID
    row_total = tap_count * chan_count + out_count
    share = row_total // shards
    chunk = share * zs + share * zs // 2
    term = in_vmem(
        functools.partial(
            weight_kernel, 1.0 / math.sqrt(dp_count * row_count * shards), tap_count, SEQ_GRID
        ),
        jax.ShapeDtypeStruct((ys * xs * chunk, LANES), jnp.bfloat16),
        7,
        KERNEL_VMEM,
        [pltpu.VMEM((row_total, LANES), jnp.float32)],
    )(normed_all, head_kept, head_got, *grad_peers)
    terms = lax.all_to_all(
        term.reshape(ys * xs, chunk, LANES),
        "seq",
        split_axis=0,
        concat_axis=0,
        tiled=True,
        axis_index_groups=[
            [(y * zs + z) * xs + x for y in range(ys) for x in range(xs)] for z in range(zs)
        ],
    )
    folded = in_vmem(
        functools.partial(fold_kernel, share, zs),
        jax.ShapeDtypeStruct((zs, 2 * share, LANES), jnp.bfloat16),
        1,
        KERNEL_VMEM,
    )(terms)
    shares = lax.all_to_all(
        folded,
        "seq",
        split_axis=0,
        concat_axis=0,
        tiled=True,
        axis_index_groups=[
            [(y * zs + z) * xs + x for z in range(zs)] for y in range(ys) for x in range(xs)
        ],
    )
    total = jnp.sum(shares.astype(jnp.float32), axis=0)
    upper = lax.axis_index("seq") // xs % zs >= zs // 2
    others = jnp.where(upper, total[share:, LANES // 2 :], total[share:, : LANES // 2])
    weight_grads = jnp.concatenate([total[:share], others], axis=1)

    input_grad = data_grad(
        activations[0], grad_above, preact_grad, grad_below, conv_weight, tap_count
    )
    return (input_grad.astype(jnp.bfloat16)[None], weight_grads)


def data_grad(inputs, grad_above, preact_grad, grad_below, conv_weight, tap_count):
    reach_rows = grad_above.shape[0]
    row_count, chan_count = inputs.shape
    input_values = inputs.astype(jnp.float32)
    norm_inverse = lax.rsqrt(
        jnp.mean(input_values * input_values, axis=1, keepdims=True) + 1e-05
    )
    grad_padded = jnp.concatenate([grad_above, preact_grad, grad_below], axis=0)
    spread = lax.dot_general(
        grad_padded, conv_weight, (((1,), (1,)), ((), ())), preferred_element_type=jnp.float32
    )
    normed_grad = spread[2 * reach_rows : 2 * reach_rows + row_count, 0:chan_count]
    for tap_index in range(1, tap_count):
        first_row = 2 * reach_rows - tap_index * DILATION
        normed_grad = (
            normed_grad
            + spread[
                first_row : first_row + row_count,
                tap_index * chan_count : (tap_index + 1) * chan_count,
            ]
        )
    return norm_inverse * normed_grad - input_values * norm_inverse**3 * jnp.mean(
        normed_grad * input_values, axis=1, keepdims=True
    )


def solution(mesh):
    placed = (
        P("dp", "seq", None),
        P(),
        P(),
        P(),
        P("dp", "seq", None),
        P("dp", "seq"),
        P("dp", "seq"),
        P("dp", "seq", None),
        P("dp", "seq"),
    )

    return jax.shard_map(
        per_device,
        mesh=mesh,
        in_specs=placed,
        out_specs=(P("dp", "seq", None), P("seq", "dp")),
        check_vma=False,
    )
```

```python
import functools
import math

import jax
import jax.numpy as jnp
from jax import lax
from jax.experimental import pallas as pl
from jax.experimental.pallas import tpu as pltpu
from jax.sharding import PartitionSpec as P


DILATION = 8
LANES = 128
SEQ_GRID = (4, 4, 4)
KERNEL_VMEM = 16 * 1024 * 1024


def gelu_slope(values):
    normal_cdf = 0.5 * (1.0 + lax.erf(values * (1.0 / math.sqrt(2.0))))
    density = jnp.exp(-0.5 * values * values) * (1.0 / math.sqrt(2.0 * math.pi))
    return normal_cdf + values * density


def contract_rows(left_side, right_side):
    return lax.dot_general(
        left_side, right_side, (((0,), (0,)), ((), ())), preferred_element_type=jnp.float32
    )


def seq_halo(cells, width):
    count = lax.axis_size("seq")
    above = lax.ppermute(cells[-width:], "seq", [(i, i + 1) for i in range(count - 1)])
    below = lax.ppermute(cells[:width], "seq", [(i + 1, i) for i in range(count - 1)])
    return above, below


def swap_core(field):
    return lax.ppermute(field, "dp", [(0, 1), (1, 0), (2, 3), (3, 2)])


def swap_z(field):
    return lax.ppermute(field, "dp", [(0, 2), (1, 3), (2, 0), (3, 1)])


def dp_columns(field, width):
    index = lax.axis_index("dp")
    found = []
    for flip in range(4):
        piece = lax.dynamic_slice_in_dim(field, (index ^ flip) * width, width, axis=1)
        if flip:
            piece = lax.ppermute(piece, "dp", [(i, i ^ flip) for i in range(4)])
        found.append(piece)
    return found


def tail_twice(values):
    return jnp.concatenate([values, values[:, LANES:]], axis=1)


def conv_kernel(taps, above_ref, below_ref, hits_ref, notes_ref, input_in, weight_ref, *rest):
    padded_out, hidden_out, slope_out, sent_ref = rest[:4]
    held_ref, input_ref, padded_ref, hidden_ref, slope_ref, done = rest[4:]
    row_count, chan_count = input_ref.shape
    input_copy = pltpu.make_async_copy(input_in, input_ref, done.at[taps + 3])
    input_copy.start()
    leaving = [
        pltpu.make_async_copy(source, target, done.at[taps + index])
        for index, (source, target) in enumerate(
            ((padded_ref, padded_out), (hidden_ref, hidden_out), (slope_ref, slope_out))
        )
    ]
    copies = []
    for k in range(taps):
        rows = pl.ds(k * chan_count, chan_count)
        copies.append(pltpu.make_async_copy(weight_ref.at[rows], held_ref.at[rows], done.at[k]))
        copies[-1].start()
    input_copy.wait()
    values = jnp.concatenate([above_ref[...], input_ref[...], below_ref[...]], axis=0).astype(
        jnp.float32
    )
    inverse = lax.rsqrt(jnp.mean(values * values, axis=1, keepdims=True) + 1e-05)
    normed = values * inverse
    padded_ref[...] = normed.astype(jnp.bfloat16)
    leaving[0].start()
    preact = jnp.zeros((row_count, hidden_ref.shape[1]), jnp.float32)
    for k in range(taps):
        column = normed[k * DILATION : k * DILATION + row_count].astype(jnp.bfloat16)
        copies[k].wait()
        preact = preact + jnp.dot(
            column,
            held_ref[k * chan_count : (k + 1) * chan_count, :],
            preferred_element_type=jnp.float32,
        )
    normal_cdf = 0.5 * (1.0 + lax.erf(preact * (1.0 / math.sqrt(2.0))))
    density = jnp.exp(-0.5 * preact * preact) * (1.0 / math.sqrt(2.0 * math.pi))
    hidden = (preact * normal_cdf).astype(jnp.bfloat16)
    hidden_ref[...] = hidden
    leaving[1].start()
    slope_ref[...] = normal_cdf + preact * density
    leaving[2].start()
    out_count = hidden_ref.shape[1]
    sent_ref[:, :out_count] = jnp.dot(
        hits_ref[...], hidden, preferred_element_type=jnp.float32
    ).astype(jnp.bfloat16)
    sent_ref[:, out_count:] = notes_ref[...]
    for copy in leaving:
        copy.wait()


def turn_kernel(own_ref, *refs):
    peers, out_ref = refs[:-1], refs[-1]
    pieces = [own_ref[...].astype(jnp.float32)]
    for peer in peers:
        pieces.append(peer[...].astype(jnp.float32))
    out_ref[...] = jnp.concatenate(pieces, axis=0).T.astype(jnp.bfloat16)


def pair_kernel(got_ref, hidden_in, first_ref, second_ref, cotangent_in, *rest):
    back_ref, part_out, feature_ref, delta_ref = rest[:4]
    hidden_ref, cotangent_ref, part_ref, done = rest[4:]
    cotangent_copy = pltpu.make_async_copy(cotangent_in, cotangent_ref, done.at[2])
    hidden_copy = pltpu.make_async_copy(hidden_in, hidden_ref, done.at[0])
    part_copy = pltpu.make_async_copy(part_ref, part_out, done.at[1])
    hidden_copy.start()
    cotangent_copy.start()
    chan_count = hidden_ref.shape[1]
    slots = got_ref.shape[0]
    note = got_ref[:, chan_count:].astype(jnp.float32)
    score = note[:, 1:2] + note[:, 2:3] + note[:, 3:4]
    row_ids = lax.broadcasted_iota(jnp.int32, (slots, hidden_ref.shape[0]), 1).astype(jnp.float32)
    hits = (note[:, 0:1] == row_ids).astype(jnp.float32).astype(jnp.bfloat16)
    hidden_copy.wait()
    accept = jnp.dot(hits, hidden_ref[...], preferred_element_type=jnp.float32)
    donor = got_ref[:, :chan_count].astype(jnp.float32)
    feature = (donor * accept).astype(jnp.bfloat16)
    feature_ref[...] = feature
    head_preact = jnp.dot(feature, first_ref[...], preferred_element_type=jnp.float32)
    delta = (score * second_ref[...].astype(jnp.float32) * gelu_slope(head_preact)).astype(
        jnp.bfloat16
    )
    delta_ref[...] = delta
    feature_grad = lax.dot_general(
        delta, first_ref[...], (((1,), (1,)), ((), ())), preferred_element_type=jnp.float32
    )
    accept_grad = (feature_grad * donor).astype(jnp.bfloat16)
    cotangent_copy.wait()
    part_ref[...] = cotangent_ref[...].astype(jnp.float32) + contract_rows(hits, accept_grad)
    part_copy.start()
    back_ref[...] = (feature_grad * accept).astype(jnp.bfloat16)
    part_copy.wait()


def head_kernel(scale, feature_ref, feature_core_ref, *refs):
    for own, core, out in zip(refs[0:2], refs[2:4], refs[4:6], strict=True):
        term = contract_rows(own[...], feature_ref[...]) + contract_rows(
            core[...], feature_core_ref[...]
        )
        out[...] = (term.T * scale).astype(jnp.bfloat16)


def weight_kernel(scale, taps, grid, *refs):
    normed_ref, heads, grads, out_ref, tail_ref = refs[0], refs[1:3], refs[3:7], refs[7], refs[8]
    ys, zs, xs = grid
    chan_count = normed_ref.shape[0]
    width = 2 * LANES
    reach = (taps - 1) * DILATION
    share = tail_ref.shape[0] // (ys * zs * xs)
    chunk = share * zs + share * zs // 2
    values = [tail_twice(ref[...].astype(jnp.float32)) for ref in grads]

    def put(first, block):
        tail_ref[first : first + block.shape[0], :] = block[:, LANES:]
        done = 0
        while done < block.shape[0]:
            owner, inside = divmod(first + done, share)
            step = min(share - inside, block.shape[0] - done)
            y, z, x = owner // (zs * xs), owner // xs % zs, owner % xs
            start = (y * xs + x) * chunk + z * share + inside
            out_ref[start : start + step, :] = block[done : done + step, :LANES].astype(jnp.bfloat16)
            done += step

    for k in range(taps):
        pieces = []
        for value in values:
            if k:
                pieces.append(jnp.zeros((k * DILATION, width), jnp.float32))
            pieces.append(value)
            if k < taps - 1:
                pieces.append(jnp.zeros((reach - k * DILATION, width), jnp.float32))
        shifted = jnp.concatenate(pieces, axis=0).astype(jnp.bfloat16)
        put(
            k * chan_count,
            jnp.dot(normed_ref[...], shifted, preferred_element_type=jnp.float32) * scale,
        )
    head_term = heads[0][...].astype(jnp.float32) + heads[1][...].astype(jnp.float32)
    put(taps * chan_count, tail_twice(head_term))
    low = lax.broadcasted_iota(jnp.int32, (share, LANES), 1) < LANES // 2
    for y in range(ys):
        for x in range(xs):
            for z in range(zs // 2):
                rows = [((y * zs + half) * xs + x) * share for half in (z, z + zs // 2)]
                start = (y * xs + x) * chunk + (zs + z) * share
                out_ref[start : start + share, :] = jnp.where(
                    low, tail_ref[rows[0] : rows[0] + share, :], tail_ref[rows[1] : rows[1] + share, :]
                ).astype(jnp.bfloat16)


def fold_kernel(share, zs, terms_ref, out_ref):
    total = terms_ref[0].astype(jnp.float32)
    for index in range(1, terms_ref.shape[0]):
        total = total + terms_ref[index].astype(jnp.float32)
    for z in range(zs):
        out_ref[z, :share, :] = total[z * share : (z + 1) * share].astype(jnp.bfloat16)
        first = (zs + z % (zs // 2)) * share
        out_ref[z, share:, :] = total[first : first + share].astype(jnp.bfloat16)


def in_hbm(field):
    return pltpu.with_memory_space_constraint(field, pltpu.HBM)


def in_vmem(kernel, shapes, count, limit, scratch=()):
    spec = pl.BlockSpec(memory_space=pltpu.VMEM)
    return pl.pallas_call(
        kernel,
        out_shape=shapes,
        in_specs=[spec] * count,
        out_specs=jax.tree.map(lambda _: spec, shapes),
        scratch_shapes=scratch,
        compiler_params=pltpu.CompilerParams(vmem_limit_bytes=limit),
    )


def per_device(
    activations,
    conv_weight,
    head_first,
    head_second,
    hidden_cotangent,
    score_cotangent,
    donor_row,
    acceptor_owner,
    acceptor_row,
):
    row_count = activations.shape[1]
    chan_count = activations.shape[2]
    out_count = conv_weight.shape[1]
    tap_count = conv_weight.shape[0] // chan_count
    reach_rows = (tap_count - 1) // 2 * DILATION
    shards = lax.axis_size("seq")
    dp_count = lax.axis_size("dp")
    pair_count = donor_row.shape[1]
    capacity = max(2, 2 * pair_count // shards)
    slots = shards * capacity
    col_width = out_count // dp_count

    above, below = seq_halo(activations[0], reach_rows)
    owner = acceptor_owner[0, :, 0]
    pair_ids = jnp.arange(pair_count, dtype=jnp.int32)
    rank = jnp.sum(
        ((owner[:, None] == owner[None, :]) & (pair_ids[None, :] < pair_ids[:, None])).astype(
            jnp.int32
        ),
        axis=1,
    )
    target = owner * capacity + rank
    placed = target[None, :] == jnp.arange(slots, dtype=jnp.int32)[:, None]
    score = score_cotangent[0]
    high = lax.reduce_precision(score, 8, 7)
    middle = lax.reduce_precision(score - high, 8, 7)
    note = jnp.stack([acceptor_row[0].astype(jnp.float32) + 1.0, high, middle, score - high - middle])
    note = jnp.pad(note, ((0, LANES - note.shape[0]), (0, 0))).astype(jnp.bfloat16)
    notes = lax.dot_general(
        placed.astype(jnp.bfloat16), note, (((1,), (1,)), ((), ())), preferred_element_type=jnp.float32
    )
    notes = (notes - (jnp.arange(LANES) == 0).astype(jnp.float32)[None, :]).astype(jnp.bfloat16)
    donor_slot = (
        jnp.sum(jnp.where(placed, donor_row[0][None, :] + 1, 0), axis=1, dtype=jnp.int32) - 1
    )
    row_ids = jnp.arange(row_count, dtype=jnp.int32)
    hits = (donor_slot[:, None] == row_ids[None, :]).astype(jnp.bfloat16)
    hits, notes = lax.optimization_barrier((hits, notes))

    spec, far = pl.BlockSpec(memory_space=pltpu.VMEM), pl.BlockSpec(memory_space=pltpu.HBM)
    padded, hidden, slope, sent = pl.pallas_call(
        functools.partial(conv_kernel, tap_count),
        out_shape=(
            pltpu.HBM((row_count + 2 * reach_rows, chan_count), jnp.bfloat16),
            pltpu.HBM((row_count, out_count), jnp.bfloat16),
            pltpu.HBM((row_count, out_count), jnp.float32),
            jax.ShapeDtypeStruct((slots, out_count + LANES), jnp.bfloat16),
        ),
        in_specs=[spec] * 4 + [far] * 2,
        out_specs=(far,) * 3 + (spec,),
        scratch_shapes=[
            pltpu.VMEM(conv_weight.shape, jnp.bfloat16),
            pltpu.VMEM((row_count, chan_count), jnp.bfloat16),
            pltpu.VMEM((row_count + 2 * reach_rows, chan_count), jnp.bfloat16),
            pltpu.VMEM((row_count, out_count), jnp.bfloat16),
            pltpu.VMEM((row_count, out_count), jnp.float32),
            pltpu.SemaphoreType.DMA((tap_count + 4,)),
        ],
        compiler_params=pltpu.CompilerParams(vmem_limit_bytes=KERNEL_VMEM),
    )(above, below, hits, notes, in_hbm(activations[0]), in_hbm(conv_weight))
    core_input, z_input = swap_core(padded), swap_z(padded)
    padded_peers = padded, core_input, z_input, swap_core(z_input)
    got = lax.all_to_all(
        sent.reshape(shards, capacity, out_count + LANES),
        "seq",
        split_axis=0,
        concat_axis=0,
        tiled=True,
    ).reshape(slots, out_count + LANES)
    slot_shape = jax.ShapeDtypeStruct((slots, out_count), jnp.bfloat16)
    back, part, feature, delta = pl.pallas_call(
        pair_kernel,
        out_shape=(
            slot_shape,
            jax.ShapeDtypeStruct((row_count, out_count), jnp.float32),
            slot_shape,
            slot_shape,
        ),
        in_specs=[spec, far, spec, spec, far],
        out_specs=(spec, far, spec, spec),
        scratch_shapes=[
            pltpu.VMEM((row_count, out_count), jnp.bfloat16),
            pltpu.VMEM((row_count, out_count), jnp.bfloat16),
            pltpu.VMEM((row_count, out_count), jnp.float32),
            pltpu.SemaphoreType.DMA((3,)),
        ],
        compiler_params=pltpu.CompilerParams(vmem_limit_bytes=KERNEL_VMEM),
    )(
        got,
        in_hbm(hidden),
        head_first,
        head_second.reshape(1, out_count),
        in_hbm(hidden_cotangent[0]),
    )
    donor_grad = lax.all_to_all(
        back.reshape(shards, capacity, out_count),
        "seq",
        split_axis=0,
        concat_axis=0,
        tiled=True,
    ).reshape(slots, out_count)
    own_place = lax.axis_index("dp")
    delta_cols = [
        lax.dynamic_slice_in_dim(delta, (own_place ^ flip) * col_width, col_width, axis=1)
        for flip in (0, 2, 1, 3)
    ]
    feature_core = swap_core(feature)
    delta_core = [swap_core(piece) for piece in delta_cols[2:]]
    head_shape = jax.ShapeDtypeStruct((out_count, col_width), jnp.bfloat16)
    head_kept, head_away = in_vmem(
        functools.partial(head_kernel, 1.0 / math.sqrt(dp_count * pair_count * shards)),
        (head_shape, head_shape),
        6,
        KERNEL_VMEM,
    )(feature, feature_core, *delta_cols[:2], *delta_core)
    head_got = swap_z(head_away)
    hidden_grad = part + contract_rows(hits, donor_grad)
    preact_grad = (hidden_grad * slope).astype(jnp.bfloat16)
    grad_peers = dp_columns(preact_grad, col_width)
    grad_above, grad_below = seq_halo(preact_grad, reach_rows)

    normed_all = in_vmem(
        turn_kernel,
        jax.ShapeDtypeStruct((chan_count, dp_count * (row_count + 2 * reach_rows)), jnp.bfloat16),
        4,
        KERNEL_VMEM,
    )(padded, *padded_peers[1:])
    ys, zs, xs = SEQ_GRID
    row_total = tap_count * chan_count + out_count
    share = row_total // shards
    chunk = share * zs + share * zs // 2
    term = in_vmem(
        functools.partial(
            weight_kernel, 1.0 / math.sqrt(dp_count * row_count * shards), tap_count, SEQ_GRID
        ),
        jax.ShapeDtypeStruct((ys * xs * chunk, LANES), jnp.bfloat16),
        7,
        KERNEL_VMEM,
        [pltpu.VMEM((row_total, LANES), jnp.float32)],
    )(normed_all, head_kept, head_got, *grad_peers)
    terms = lax.all_to_all(
        term.reshape(ys * xs, chunk, LANES),
        "seq",
        split_axis=0,
        concat_axis=0,
        tiled=True,
        axis_index_groups=[
            [(y * zs + z) * xs + x for y in range(ys) for x in range(xs)] for z in range(zs)
        ],
    )
    folded = in_vmem(
        functools.partial(fold_kernel, share, zs),
        jax.ShapeDtypeStruct((zs, 2 * share, LANES), jnp.bfloat16),
        1,
        KERNEL_VMEM,
    )(terms)
    shares = lax.all_to_all(
        folded,
        "seq",
        split_axis=0,
        concat_axis=0,
        tiled=True,
        axis_index_groups=[
            [(y * zs + z) * xs + x for z in range(zs)] for y in range(ys) for x in range(xs)
        ],
    )
    total = jnp.sum(shares.astype(jnp.float32), axis=0)
    upper = lax.axis_index("seq") // xs % zs >= zs // 2
    others = jnp.where(upper, total[share:, LANES // 2 :], total[share:, : LANES // 2])
    weight_grads = jnp.concatenate([total[:share], others], axis=1)

    input_grad = data_grad(
        activations[0], grad_above, preact_grad, grad_below, conv_weight, tap_count
    )
    return (input_grad.astype(jnp.bfloat16)[None], weight_grads)


def data_grad(inputs, grad_above, preact_grad, grad_below, conv_weight, tap_count):
    reach_rows = grad_above.shape[0]
    row_count, chan_count = inputs.shape
    input_values = inputs.astype(jnp.float32)
    norm_inverse = lax.rsqrt(
        jnp.mean(input_values * input_values, axis=1, keepdims=True) + 1e-05
    )
    grad_padded = jnp.concatenate([grad_above, preact_grad, grad_below], axis=0)
    spread = lax.dot_general(
        grad_padded, conv_weight, (((1,), (1,)), ((), ())), preferred_element_type=jnp.float32
    )
    normed_grad = spread[2 * reach_rows : 2 * reach_rows + row_count, 0:chan_count]
    for tap_index in range(1, tap_count):
        first_row = 2 * reach_rows - tap_index * DILATION
        normed_grad = (
            normed_grad
            + spread[
                first_row : first_row + row_count,
                tap_index * chan_count : (tap_index + 1) * chan_count,
            ]
        )
    return norm_inverse * normed_grad - input_values * norm_inverse**3 * jnp.mean(
        normed_grad * input_values, axis=1, keepdims=True
    )


def solution(mesh):
    placed = (
        P("dp", "seq", None),
        P(),
        P(),
        P(),
        P("dp", "seq", None),
        P("dp", "seq"),
        P("dp", "seq"),
        P("dp", "seq", None),
        P("dp", "seq"),
    )

    return jax.shard_map(
        per_device,
        mesh=mesh,
        in_specs=placed,
        out_specs=(P("dp", "seq", None), P("seq", "dp")),
        check_vma=False,
    )
```
